32 devices in a mesh: pairs: 2 (over y), lon: 4 (over z), grp: 4 (over x, core).
Axes of the slice: x: 2, y: 2, z: 4, core: 2. Of those that a mesh axis runs over, the one named last changes fastest.
Arguments:
- left_feats: bfloat16 [320, 32, 256], P('grp', 'pairs', 'lon'), parts along dimension 1, may hold values from -12 to 12
- right_feats: bfloat16 [320, 32, 256], P('grp', 'pairs', 'lon'), parts along dimension 1, may hold values from -12 to 12
- w_first: bfloat16 [32, 40, 3, 3, 3], replicated, may hold values from -0.1875 to 0.1875
- w_second: bfloat16 [32, 32, 3, 3, 3], replicated, may hold values from -0.21875 to 0.21875
- w_out: bfloat16 [1, 32, 3, 3, 3], replicated, may hold values from -0.81640625 to 0.81640625
Outputs:
- disparity: float32 [32, 256], P(('pairs', 'grp'), 'lon'), parts along dimension 0
The draws below stay inside these ranges and needn't reach their ends.
There are 2 independent parts, one for each index of `pairs`. The reference program is written for one: setup_inputs(seed, part) draws one part's arguments, and reference() takes and returns one part's arrays. A program takes and returns all parts, laid end to end along the dimension named above; an argument that names none is the same for every part. Nothing has to cross between parts.
All inputs are finite; a program needn't handle non-finite values.
Results may differ from the reference program's by a relative error of at most 0.0041.
Values may be sent and summed in bfloat16 or wider, within the bound.
No kernel may reach another device: no remote copies, remote signals or barrier semaphores. Data moves between devices by JAX's collectives and lax.ppermute only.
A program may use at most 64 MiB of HBM per device.

```python
import jax
import jax.numpy as jnp
from jax import lax

C = 320
G = 40
CH = 32
DISP = 48
ROWS = 16
W = 256


def block_levels(stream_key, dims, cuts, low, top_value):
    gain, own = 1.0, jax.random.fold_in(stream_key, 6)
    for axis_at, shards_of in cuts:
        steps = jnp.exp(jax.random.uniform(jax.random.fold_in(own, axis_at), (shards_of,), jnp.float32, low / len(cuts), top_value / len(cuts)))
        gain = gain * jnp.repeat(steps, dims[axis_at] // shards_of).reshape([-1 if axis == axis_at else 1 for axis in range(len(dims))])
    return gain


def gaussian(stream_key, extent, deviation, limit, shards=(), kind=jnp.bfloat16):
    values = jax.random.normal(stream_key, extent, jnp.float32) * deviation
    if len(shards) > 0:
        values = block_levels(stream_key, extent, shards, -0.22, 0.18) * values
    return jnp.clip(values, min=-limit, max=limit).astype(kind)


def setup_inputs(seed: int = 0, part: int = 0) -> dict:
    streams_of = jax.random.split(jax.random.key(seed), 6)
    part_splits = jax.random.split(jax.random.fold_in(streams_of[5], part), 6)
    return {
        "left_feats": gaussian(part_splits[0], (C, ROWS, W), 2.0, 12.0, ((0, 4), (2, 4))),
        "right_feats": gaussian(part_splits[1], (C, ROWS, W), 2.0, 12.0, ((0, 4), (2, 4))),
        "w_first": gaussian(streams_of[2], (CH, G, 3, 3, 3), (G * 27) ** -0.5, 0.1875),
        "w_second": gaussian(streams_of[3], (CH, CH, 3, 3, 3), (CH * 27) ** -0.5, 0.21875),
        "w_out": gaussian(streams_of[4], (1, CH, 3, 3, 3), (4.0 / (CH * 27) ** 0.5), 0.81640625),
    }


logit_cap = 12.0


def convolve_full(volume, kernel, dilation):
    wrapped = jnp.concatenate([volume[..., -dilation:], volume, volume[..., :dilation]], axis=3)
    padded = jnp.pad(wrapped, ((0, 0), (dilation, dilation), (dilation, dilation), (0, 0)))
    result = lax.conv_general_dilated(padded[None], kernel.astype(jnp.float32), (1, 1, 1), "VALID", rhs_dilation=(dilation, dilation, dilation), dimension_numbers=("NCDHW", "OIDHW", "NCDHW"))
    return result[0]


def reference(left_feats, right_feats, w_first, w_second, w_out):
    channels, row_count, col_count = left_feats.shape
    group_size = C // G
    left_wide = left_feats.astype(jnp.float32)
    right_wide = right_feats.astype(jnp.float32)
    slices = []
    for shift_by in range(DISP):
        shifted = jnp.roll(right_wide, shift_by, axis=2)
        products = (left_wide * shifted).reshape(G, group_size, row_count, col_count)
        slices.append(jnp.sum(products, axis=1) / group_size)
    cost = lax.optimization_barrier(jnp.stack(slices, axis=1).astype(jnp.bfloat16))
    first_layer = jax.nn.relu(convolve_full(cost.astype(jnp.float32), w_first, 1)).astype(jnp.bfloat16)
    first_layer = lax.optimization_barrier(first_layer)
    first_wide = first_layer.astype(jnp.float32)
    second_layer = jax.nn.relu(convolve_full(first_wide, w_second, 2) + first_wide).astype(jnp.bfloat16)
    second_layer = lax.optimization_barrier(second_layer)
    scores = convolve_full(second_layer.astype(jnp.float32), w_out, 1)[0]
    capped = logit_cap * jnp.tanh(scores / logit_cap)
    weights = jnp.exp(capped)
    levels = jnp.arange(DISP).astype(jnp.float32)[:, None, None]
    return jnp.sum(weights * levels, axis=0) / jnp.sum(weights, axis=0) / DISP
```

```python
import functools

import jax
import jax.numpy as jnp
from jax import lax
from jax.experimental import pallas as pl
from jax.experimental.pallas import tpu as pltpu
from jax.sharding import PartitionSpec as P

C = 320
G = 40
CH = 32
DISP = 48
PER = C // G
ROWS = 16
HALF = ROWS // 2
LANE = 128
HALO = 4
SPREAD = DISP - 1
FIRST_IN = G * ROWS
FIRST_OUT = ROWS * CH
PART = FIRST_OUT // 2
CAP = 12.0


def weights_kernel(order_ref, v1_ref, v2_ref, v3_ref, t1_ref, t2_ref, t3_ref, *, slots):
    here = G // slots
    row16 = lax.broadcasted_iota(jnp.int32, (ROWS, LANE), 0)
    quarter = lax.broadcasted_iota(jnp.int32, (ROWS, LANE), 1) // CH
    masks = []
    for q in range(FIRST_OUT // LANE):
        at = 4 * q + quarter
        out_row = 2 * (at % HALF) + at // HALF
        masks.append([row16 == out_row + kh - 1 for kh in range(3)])

    def tap(t, carry):
        kw, e = t // 3, t % 3

        def one_group(i, carry):
            group = order_ref[i // here] * here + i % here
            rows = [
                jnp.broadcast_to(v1_ref[t, kh, pl.ds(group, 1), :], (ROWS, LANE)) for kh in range(3)
            ]
            start = pl.multiple_of(e * FIRST_IN + i * ROWS, ROWS)
            for q in range(FIRST_OUT // LANE):
                value = jnp.zeros((ROWS, LANE), jnp.float32)
                for kh in range(3):
                    value = jnp.where(masks[q][kh], rows[kh], value)
                t1_ref[kw, pl.ds(start, ROWS), q * LANE : (q + 1) * LANE] = value.astype(jnp.bfloat16)
            return carry

        lax.fori_loop(0, G, one_group, 0)
        lane32 = lax.broadcasted_iota(jnp.int32, (CH, LANE), 1) // CH
        for hi in range(HALF):
            start = pl.multiple_of(e * PART + hi * CH, CH)
            for q in range(PART // LANE):
                value = jnp.zeros((CH, LANE), jnp.float32)
                for kh in range(3):
                    value = jnp.where(4 * q + lane32 == hi - kh + 1, v2_ref[t, kh], value)
                t2_ref[kw, pl.ds(start, CH), q * LANE : (q + 1) * LANE] = value.astype(jnp.bfloat16)
        return carry

    lax.fori_loop(0, 9, tap, 0)
    out16 = lax.broadcasted_iota(jnp.int32, (CH, LANE), 1) % ROWS
    for kw in range(3):
        for at in range(ROWS):
            hi = 2 * (at % HALF) + at // HALF
            value = jnp.zeros((CH, LANE), jnp.float32)
            for kh in range(3):
                value = jnp.where(out16 == hi - kh + 1, v3_ref[kw * 3 + kh], value)
            t3_ref[kw, at * CH : (at + 1) * CH, :] = value.astype(jnp.bfloat16)


def banded_weights(order, w_first, w_second, w_out, slots):
    v1 = jnp.transpose(w_first[:, :, ::-1], (4, 2, 3, 1, 0)).astype(jnp.float32)
    v1 = jnp.tile(v1.reshape(9, 3, G, CH), (1, 1, 1, 4))
    v2 = jnp.transpose(w_second[:, :, ::-1], (4, 2, 3, 1, 0)).astype(jnp.float32)
    v2 = jnp.tile(v2.reshape(9, 3, CH, CH), (1, 1, 1, 4))
    v3 = jnp.transpose(w_out[0, :, ::-1], (3, 2, 0, 1)).astype(jnp.float32)
    v3 = jnp.repeat(v3, ROWS, axis=3)
    v3 = jnp.pad(v3, ((0, 0), (0, 0), (0, 0), (0, LANE - 3 * ROWS))).reshape(9, CH, LANE)
    whole = pl.BlockSpec(memory_space=pltpu.VMEM)
    return pl.pallas_call(
        functools.partial(weights_kernel, slots=slots),
        out_shape=(
            jax.ShapeDtypeStruct((3, 3 * FIRST_IN, FIRST_OUT), jnp.bfloat16),
            jax.ShapeDtypeStruct((3, 3 * PART, PART), jnp.bfloat16),
            jax.ShapeDtypeStruct((3, FIRST_OUT, LANE), jnp.bfloat16),
        ),
        in_specs=[pl.BlockSpec(memory_space=pltpu.SMEM), whole, whole, whole],
        out_specs=[whole, whole, whole],
        compiler_params=pltpu.CompilerParams(vmem_limit_bytes=20 << 20),
        cost_estimate=pl.CostEstimate(flops=9_000_000, bytes_accessed=8_000_000, transcendentals=0),
        name="banded_weights",
    )(order, v1, v2, v3)


def main_kernel(
    feats_ref, t1_hbm, t2_ref, t3_ref, out_ref,
    t1_ref, left, right, cells, cost_pad, acc1, first, first_pad, second, score_pad, sem,
    *, slots, cols,
):
    fetch = pltpu.make_async_copy(t1_hbm, t1_ref, sem)
    fetch.start()
    here = G // slots
    span = here * ROWS
    cost_cols, first_cols, second_cols = cols + 8, cols + 6, cols + 2
    right_rows = cost_cols + SPREAD
    blocks = FIRST_IN // LANE
    for k in range(PER):
        pieces = [
            feats_ref[s, :, k * span : (k + 1) * span].astype(jnp.float32) for s in range(slots)
        ]
        joined = jnp.concatenate(pieces, axis=1)
        for j in range(blocks):
            tile = joined[:, j * LANE : (j + 1) * LANE]
            left[k * blocks + j, :, :] = tile[:cost_cols]
            right[k * blocks + j, :, :] = tile[cost_cols:]

    for ref in (cost_pad, first_pad, score_pad):
        ref[...] = jnp.zeros_like(ref)

    def cost_column(w, carry):
        base = pl.multiple_of(w * DISP, DISP)
        for j in range(blocks):
            total = None
            for k in range(PER):
                at = k * blocks + j
                l_row = jnp.broadcast_to(left[at, pl.ds(w, 1), :], (DISP, LANE))
                term = l_row * right[at, pl.ds(w, DISP), :]
                total = term if total is None else total + term
            total = (total * (1.0 / PER)).astype(jnp.bfloat16)
            cost_pad[j, 8 : 8 + DISP, :] = total.astype(jnp.float32)
            for e in range(3):
                lanes = e * FIRST_IN + j * LANE
                if e == 1:
                    moved = total
                else:
                    moved = cost_pad[j, 7 + e : 7 + e + DISP, :].astype(jnp.bfloat16)
                cells[pl.ds(base, DISP), lanes : lanes + LANE] = moved
        return carry

    lax.fori_loop(0, cost_cols, cost_column, 0)
    fetch.wait()

    half1 = first_cols // 2

    def first_half(part, carry):
        for kw in range(3):
            start = pl.multiple_of((part * half1 + kw) * DISP, DISP)
            term = jnp.dot(
                cells[pl.ds(start, half1 * DISP), :], t1_ref[kw], preferred_element_type=jnp.float32
            )
            if kw == 0:
                acc1[...] = term
            else:
                acc1[...] += term

        def column(w, carry):
            local = pl.multiple_of(w * DISP, DISP)
            base = pl.multiple_of((part * half1 + w) * DISP, DISP)
            for q in range(FIRST_OUT // LANE):
                value = acc1[pl.ds(local, DISP), q * LANE : (q + 1) * LANE]
                value = jnp.maximum(value, 0.0).astype(jnp.bfloat16)
                first_pad[q, 8 : 8 + DISP, :] = value.astype(jnp.float32)
                for e in range(3):
                    lanes = (q // 2) * 3 * PART + e * PART + (q % 2) * LANE
                    if e == 1:
                        moved = value
                    else:
                        moved = first_pad[q, 6 + 2 * e : 6 + 2 * e + DISP, :].astype(jnp.bfloat16)
                    first[pl.ds(base, DISP), lanes : lanes + LANE] = moved
            return carry

        lax.fori_loop(0, half1, column, 0)
        return carry

    lax.fori_loop(0, 2, first_half, 0)

    half2 = second_cols // 2

    def second_half(part, carry):
        out_at = pl.multiple_of(part * half2 * DISP, DISP)
        for p in range(2):
            lanes = p * 3 * PART
            total = None
            for kw in range(3):
                start = pl.multiple_of((part * half2 + 2 * kw) * DISP, DISP)
                term = jnp.dot(
                    first[pl.ds(start, half2 * DISP), lanes : lanes + 3 * PART],
                    t2_ref[kw],
                    preferred_element_type=jnp.float32,
                )
                total = term if total is None else total + term
            start = pl.multiple_of((part * half2 + 2) * DISP, DISP)
            kept = first[pl.ds(start, half2 * DISP), lanes + PART : lanes + 2 * PART]
            total = jnp.maximum(total + kept.astype(jnp.float32), 0.0).astype(jnp.bfloat16)
            second[pl.ds(out_at, half2 * DISP), p * PART : (p + 1) * PART] = total
        return carry

    lax.fori_loop(0, 2, second_half, 0)

    level = (DISP - 1) - lax.broadcasted_iota(jnp.int32, (DISP, LANE), 0)
    level = level.astype(jnp.float32)

    def score_column(w, carry):
        total = None
        for kw in range(3):
            start = pl.multiple_of((w + kw) * DISP, DISP)
            term = jnp.dot(
                second[pl.ds(start, DISP), :], t3_ref[kw], preferred_element_type=jnp.float32
            )
            total = term if total is None else total + term
        score_pad[8 : 8 + DISP, :] = total
        score = score_pad[7 : 7 + DISP, :]
        score = score + pltpu.roll(total, LANE - ROWS, 1)
        score = score + pltpu.roll(score_pad[9 : 9 + DISP, :], LANE - 2 * ROWS, 1)
        weights = jnp.exp(CAP * jnp.tanh(score / CAP))
        bottom = jnp.sum(weights, axis=0, keepdims=True)
        top = jnp.sum(weights * level, axis=0, keepdims=True)
        out_ref[pl.ds(w, 1), :] = top / bottom / DISP
        return carry

    lax.fori_loop(0, cols, score_column, 0)


def aggregate(feats, t1, t2, t3, slots, cols):
    cost_cols, first_cols, second_cols = cols + 8, cols + 6, cols + 2
    right_rows = cost_cols + SPREAD
    whole = pl.BlockSpec(memory_space=pltpu.VMEM)
    tiles = PER * FIRST_IN // LANE
    return pl.pallas_call(
        functools.partial(main_kernel, slots=slots, cols=cols),
        out_shape=jax.ShapeDtypeStruct((cols, LANE), jnp.float32),
        in_specs=[whole, pl.BlockSpec(memory_space=pl.ANY), whole, whole],
        out_specs=whole,
        scratch_shapes=[
            pltpu.VMEM((3, 3 * FIRST_IN, FIRST_OUT), jnp.bfloat16),
            pltpu.VMEM((tiles, cost_cols, LANE), jnp.float32),
            pltpu.VMEM((tiles, right_rows, LANE), jnp.float32),
            pltpu.VMEM((cost_cols * DISP, 3 * FIRST_IN), jnp.bfloat16),
            pltpu.VMEM((FIRST_IN // LANE, DISP + 16, LANE), jnp.float32),
            pltpu.VMEM((first_cols // 2 * DISP, FIRST_OUT), jnp.float32),
            pltpu.VMEM((first_cols * DISP, 3 * FIRST_OUT), jnp.bfloat16),
            pltpu.VMEM((FIRST_OUT // LANE, DISP + 16, LANE), jnp.float32),
            pltpu.VMEM((second_cols * DISP, FIRST_OUT), jnp.bfloat16),
            pltpu.VMEM((DISP + 16, LANE), jnp.float32),
            pltpu.SemaphoreType.DMA,
        ],
        compiler_params=pltpu.CompilerParams(vmem_limit_bytes=40 << 20),
        name="aggregate",
    )(feats, t1, t2, t3)


def by_column(block):
    channels, row_count, col_count = block.shape
    grouped = block.reshape(channels // PER, PER, row_count, col_count)
    return jnp.transpose(grouped, (3, 1, 0, 2)).reshape(col_count, channels * row_count)


def passed(value, axis, by):
    peers = lax.axis_size(axis)
    return lax.ppermute(value, axis, [(i, (i + by) % peers) for i in range(peers)])


def per_device(left_feats, right_feats, w_first, w_second, w_out):
    channels, row_count, col_count = left_feats.shape
    slots = lax.axis_size("grp")
    me = lax.axis_index("grp")
    cols = col_count // slots
    left, right = by_column(left_feats), by_column(right_feats)
    behind = HALO + SPREAD
    ahead = passed(
        jnp.concatenate([right[col_count - behind :], left[col_count - HALO :]], axis=0), "lon", 1
    )
    after = passed(jnp.concatenate([right[:HALO], left[:HALO]], axis=0), "lon", -1)
    left_wide = jnp.concatenate([ahead[behind:], left, after[HALO:]], axis=0)
    right_wide = jnp.concatenate([ahead[:behind], right, after[:HALO]], axis=0)
    windows = jnp.stack(
        [
            jnp.concatenate(
                [
                    left_wide[j * cols : j * cols + cols + 2 * HALO],
                    right_wide[j * cols : j * cols + cols + 2 * HALO + SPREAD],
                ],
                axis=0,
            )
            for j in range(slots)
        ]
    )
    feats = lax.all_to_all(windows, "grp", split_axis=0, concat_axis=0, tiled=True)
    order = jnp.arange(slots, dtype=jnp.int32)
    t1, t2, t3 = banded_weights(order, w_first, w_second, w_out, slots)
    part = aggregate(feats, t1, t2, t3, slots, cols)[:, :ROWS]
    share = row_count // slots
    split = part.reshape(cols, slots, share)
    rows = [lax.dynamic_index_in_dim(split, me, 1, keepdims=False)]
    for by in range(1, slots):
        target = (me + by) % slots
        rows.append(passed(lax.dynamic_index_in_dim(split, target, 1, keepdims=False), "grp", by))
    gathered = jnp.concatenate(rows, axis=0).reshape(slots, cols, share)
    placed = jnp.zeros_like(gathered)
    for by in range(slots):
        placed = lax.dynamic_update_index_in_dim(placed, gathered[by], (me - by) % slots, 0)
    return placed.reshape(col_count, share).T


def solution(mesh):
    placed = (P("grp", "pairs", "lon"), P("grp", "pairs", "lon"), P(), P(), P())
    return jax.shard_map(
        per_device,
        mesh=mesh,
        in_specs=placed,
        out_specs=P(("pairs", "grp"), "lon"),
        check_vma=False,
    )
```

```python
import functools

import jax
import jax.numpy as jnp
from jax import lax
from jax.experimental import pallas as pl
from jax.experimental.pallas import tpu as pltpu
from jax.sharding import PartitionSpec as P

C = 320
G = 40
CH = 32
DISP = 48
PER = C // G
ROWS = 16
HALF = ROWS // 2
LANE = 128
HALO = 4
SPREAD = DISP - 1
FIRST_IN = G * ROWS
FIRST_OUT = ROWS * CH
PART = FIRST_OUT // 2
CAP = 12.0


def weights_kernel(
    order_ref, w1_ref, w2_ref, w3_ref, t1_hbm, t2_hbm, t3_hbm, t1_ref, t2_ref, t3_ref, v1, sems, *, slots
):
    here = G // slots
    quarters = LANE // CH
    for tap in range(27):
        w1 = w1_ref[tap].astype(jnp.float32)
        v1[tap, :, :] = jnp.transpose(jnp.concatenate([w1] * quarters, axis=0))
    row16 = lax.broadcasted_iota(jnp.int32, (ROWS, LANE), 0)
    quarter = lax.broadcasted_iota(jnp.int32, (ROWS, LANE), 1) // CH
    masks = []
    for q in range(FIRST_OUT // LANE):
        at = quarters * q + quarter
        out_row = 2 * (at % HALF) + at // HALF
        masks.append(
            [jnp.where(row16 == out_row + kh - 1, 1.0, 0.0).astype(jnp.bfloat16) for kh in range(3)]
        )
    for kw in range(3):

        def one_tap(t, carry):
            e, slot = t // slots, t % slots
            tap = (2 - e) * 9 + kw
            group = order_ref[slot] * here
            for i in range(here):
                rows = []
                for kh in range(3):
                    row = v1[tap + 3 * kh, pl.ds(group + i, 1), :]
                    rows.append(jnp.broadcast_to(row, (ROWS, LANE)).astype(jnp.bfloat16))
                start = pl.multiple_of(e * FIRST_IN + (slot * here + i) * ROWS, ROWS)
                for q in range(FIRST_OUT // LANE):
                    value = masks[q][0] * rows[0] + masks[q][1] * rows[1] + masks[q][2] * rows[2]
                    t1_ref[kw, pl.ds(start, ROWS), q * LANE : (q + 1) * LANE] = value
            return carry

        lax.fori_loop(0, 3 * slots, one_tap, 0)
        pltpu.make_async_copy(t1_ref.at[kw], t1_hbm.at[kw], sems.at[kw]).start()

    lane32 = lax.broadcasted_iota(jnp.int32, (CH, LANE), 1) // CH
    for kw in range(3):
        for e in range(3):
            tap = (2 - e) * 9 + kw
            v2 = [
                jnp.transpose(
                    jnp.concatenate([w2_ref[tap + 3 * kh].astype(jnp.float32)] * quarters, axis=0)
                )
                for kh in range(3)
            ]
            for hi in range(HALF):
                for q in range(PART // LANE):
                    value = jnp.zeros((CH, LANE), jnp.float32)
                    for kh in range(3):
                        if quarters * q <= hi - kh + 1 < quarters * (q + 1):
                            value = jnp.where(quarters * q + lane32 == hi - kh + 1, v2[kh], value)
                    start = e * PART + hi * CH
                    t2_ref[kw, start : start + CH, q * LANE : (q + 1) * LANE] = value.astype(
                        jnp.bfloat16
                    )
    pltpu.make_async_copy(t2_ref, t2_hbm, sems.at[3]).start()

    out_lane = lax.broadcasted_iota(jnp.int32, (CH, LANE), 1)
    for kw in range(3):
        v3 = []
        for kh in range(3):
            value = jnp.zeros((CH, LANE), jnp.float32)
            for e in range(3):
                tap = (2 - e) * 9 + 3 * kh + kw
                column = jnp.broadcast_to(w3_ref[:, tap : tap + 1], (CH, LANE))
                value = jnp.where(out_lane // ROWS == e, column, value)
            v3.append(value)
        for at in range(ROWS):
            hi = 2 * (at % HALF) + at // HALF
            value = jnp.zeros((CH, LANE), jnp.float32)
            for kh in range(3):
                value = jnp.where(out_lane % ROWS == hi - kh + 1, v3[kh], value)
            t3_ref[kw, at * CH : (at + 1) * CH, :] = value.astype(jnp.bfloat16)
    pltpu.make_async_copy(t3_ref, t3_hbm, sems.at[4]).start()
    for kw in range(3):
        pltpu.make_async_copy(t1_ref.at[kw], t1_hbm.at[kw], sems.at[kw]).wait()
    pltpu.make_async_copy(t2_ref, t2_hbm, sems.at[3]).wait()
    pltpu.make_async_copy(t3_ref, t3_hbm, sems.at[4]).wait()


def banded_weights(order, w_first, w_second, w_out, slots):
    w1 = jnp.transpose(w_first, (2, 3, 4, 0, 1)).reshape(27, CH, G)
    w2 = jnp.transpose(w_second, (2, 3, 4, 0, 1)).reshape(27, CH, CH)
    w3 = w_out.reshape(CH, 27).astype(jnp.float32)
    whole = pl.BlockSpec(memory_space=pltpu.VMEM)
    far = pl.BlockSpec(memory_space=pltpu.HBM)
    shapes = [
        (3, 3 * FIRST_IN, FIRST_OUT),
        (3, 3 * PART, PART),
        (3, FIRST_OUT, LANE),
    ]
    return pl.pallas_call(
        functools.partial(weights_kernel, slots=slots),
        out_shape=tuple(jax.ShapeDtypeStruct(shape, jnp.bfloat16) for shape in shapes),
        in_specs=[pl.BlockSpec(memory_space=pltpu.SMEM), whole, whole, whole],
        out_specs=[far, far, far],
        scratch_shapes=[pltpu.VMEM(shape, jnp.bfloat16) for shape in shapes]
        + [pltpu.VMEM((27, G, LANE), jnp.float32), pltpu.SemaphoreType.DMA((5,))],
        compiler_params=pltpu.CompilerParams(vmem_limit_bytes=59 << 20),
        cost_estimate=pl.CostEstimate(flops=9_000_000, bytes_accessed=8_000_000, transcendentals=0),
        name="banded_weights",
    )(order, w1, w2, w3)


def main_kernel(
    feats_ref, t1_hbm, t2_hbm, t3_hbm, out_ref,
    t1_ref, t2_ref, t3_ref, left, right, cells, cost_pad, acc1, first, first_pad, second, score_pad, sems,
    *, slots, cols,
):
    fetches = [
        pltpu.make_async_copy(t1_hbm, t1_ref, sems.at[0]),
        pltpu.make_async_copy(t2_hbm, t2_ref, sems.at[1]),
        pltpu.make_async_copy(t3_hbm, t3_ref, sems.at[2]),
    ]
    for fetch in fetches:
        fetch.start()
    here = G // slots
    span = here * ROWS
    cost_cols, first_cols, second_cols = cols + 8, cols + 6, cols + 2
    right_rows = cost_cols + SPREAD
    blocks = FIRST_IN // LANE
    for k in range(PER):
        pieces = [
            feats_ref[s, :, k * span : (k + 1) * span].astype(jnp.float32) for s in range(slots)
        ]
        joined = jnp.concatenate(pieces, axis=1)
        for j in range(blocks):
            tile = joined[:, j * LANE : (j + 1) * LANE]
            left[k * blocks + j, :, :] = tile[:cost_cols]
            right[k * blocks + j, :, :] = tile[cost_cols:]

    for ref in (cost_pad, first_pad, score_pad):
        ref[...] = jnp.zeros_like(ref)

    def cost_column(w, carry):
        base = pl.multiple_of(w * DISP, DISP)
        for j in range(blocks):
            total = None
            for k in range(PER):
                at = k * blocks + j
                l_row = jnp.broadcast_to(left[at, pl.ds(w, 1), :], (DISP, LANE))
                term = l_row * right[at, pl.ds(w, DISP), :]
                total = term if total is None else total + term
            total = (total * (1.0 / PER)).astype(jnp.bfloat16)
            cost_pad[j, 8 : 8 + DISP, :] = total.astype(jnp.float32)
            for e in range(3):
                lanes = e * FIRST_IN + j * LANE
                if e == 1:
                    moved = total
                else:
                    moved = cost_pad[j, 7 + e : 7 + e + DISP, :].astype(jnp.bfloat16)
                cells[pl.ds(base, DISP), lanes : lanes + LANE] = moved
        return carry

    lax.fori_loop(0, cost_cols, cost_column, 0)
    for fetch in fetches:
        fetch.wait()

    half1 = first_cols // 2

    def first_half(part, carry):
        for kw in range(3):
            start = pl.multiple_of((part * half1 + kw) * DISP, DISP)
            term = jnp.dot(
                cells[pl.ds(start, half1 * DISP), :], t1_ref[kw], preferred_element_type=jnp.float32
            )
            if kw == 0:
                acc1[...] = term
            else:
                acc1[...] += term

        def column(w, carry):
            local = pl.multiple_of(w * DISP, DISP)
            base = pl.multiple_of((part * half1 + w) * DISP, DISP)
            for q in range(FIRST_OUT // LANE):
                value = acc1[pl.ds(local, DISP), q * LANE : (q + 1) * LANE]
                value = jnp.maximum(value, 0.0).astype(jnp.bfloat16)
                first_pad[q, 8 : 8 + DISP, :] = value.astype(jnp.float32)
                for e in range(3):
                    lanes = (q // 2) * 3 * PART + e * PART + (q % 2) * LANE
                    if e == 1:
                        moved = value
                    else:
                        moved = first_pad[q, 6 + 2 * e : 6 + 2 * e + DISP, :].astype(jnp.bfloat16)
                    first[pl.ds(base, DISP), lanes : lanes + LANE] = moved
            return carry

        lax.fori_loop(0, half1, column, 0)
        return carry

    lax.fori_loop(0, 2, first_half, 0)

    half2 = second_cols // 2

    def second_half(part, carry):
        out_at = pl.multiple_of(part * half2 * DISP, DISP)
        for p in range(2):
            lanes = p * 3 * PART
            total = None
            for kw in range(3):
                start = pl.multiple_of((part * half2 + 2 * kw) * DISP, DISP)
                term = jnp.dot(
                    first[pl.ds(start, half2 * DISP), lanes : lanes + 3 * PART],
                    t2_ref[kw],
                    preferred_element_type=jnp.float32,
                )
                total = term if total is None else total + term
            start = pl.multiple_of((part * half2 + 2) * DISP, DISP)
            kept = first[pl.ds(start, half2 * DISP), lanes + PART : lanes + 2 * PART]
            total = jnp.maximum(total + kept.astype(jnp.float32), 0.0).astype(jnp.bfloat16)
            second[pl.ds(out_at, half2 * DISP), p * PART : (p + 1) * PART] = total
        return carry

    lax.fori_loop(0, 2, second_half, 0)

    level = (DISP - 1) - lax.broadcasted_iota(jnp.int32, (DISP, LANE), 0)
    level = level.astype(jnp.float32)

    def score_column(w, carry):
        total = None
        for kw in range(3):
            start = pl.multiple_of((w + kw) * DISP, DISP)
            term = jnp.dot(
                second[pl.ds(start, DISP), :], t3_ref[kw], preferred_element_type=jnp.float32
            )
            total = term if total is None else total + term
        score_pad[8 : 8 + DISP, :] = total
        score = score_pad[7 : 7 + DISP, :]
        score = score + pltpu.roll(total, LANE - ROWS, 1)
        score = score + pltpu.roll(score_pad[9 : 9 + DISP, :], LANE - 2 * ROWS, 1)
        weights = jnp.exp(CAP * jnp.tanh(score / CAP))
        bottom = jnp.sum(weights, axis=0, keepdims=True)
        top = jnp.sum(weights * level, axis=0, keepdims=True)
        out_ref[pl.ds(w, 1), :] = top / bottom / DISP
        return carry

    lax.fori_loop(0, cols, score_column, 0)


def aggregate(feats, t1, t2, t3, slots, cols):
    cost_cols, first_cols, second_cols = cols + 8, cols + 6, cols + 2
    right_rows = cost_cols + SPREAD
    whole = pl.BlockSpec(memory_space=pltpu.VMEM)
    far = pl.BlockSpec(memory_space=pltpu.HBM)
    tiles = PER * FIRST_IN // LANE
    return pl.pallas_call(
        functools.partial(main_kernel, slots=slots, cols=cols),
        out_shape=jax.ShapeDtypeStruct((cols, LANE), jnp.float32),
        in_specs=[whole, far, far, far],
        out_specs=whole,
        scratch_shapes=[
            pltpu.VMEM((3, 3 * FIRST_IN, FIRST_OUT), jnp.bfloat16),
            pltpu.VMEM((3, 3 * PART, PART), jnp.bfloat16),
            pltpu.VMEM((3, FIRST_OUT, LANE), jnp.bfloat16),
            pltpu.VMEM((tiles, cost_cols, LANE), jnp.float32),
            pltpu.VMEM((tiles, right_rows, LANE), jnp.float32),
            pltpu.VMEM((cost_cols * DISP, 3 * FIRST_IN), jnp.bfloat16),
            pltpu.VMEM((FIRST_IN // LANE, DISP + 16, LANE), jnp.float32),
            pltpu.VMEM((first_cols // 2 * DISP, FIRST_OUT), jnp.float32),
            pltpu.VMEM((first_cols * DISP, 3 * FIRST_OUT), jnp.bfloat16),
            pltpu.VMEM((FIRST_OUT // LANE, DISP + 16, LANE), jnp.float32),
            pltpu.VMEM((second_cols * DISP, FIRST_OUT), jnp.bfloat16),
            pltpu.VMEM((DISP + 16, LANE), jnp.float32),
            pltpu.SemaphoreType.DMA((3,)),
        ],
        compiler_params=pltpu.CompilerParams(vmem_limit_bytes=57 << 20),
        name="aggregate",
    )(feats, t1, t2, t3)


def by_column(block):
    channels, row_count, col_count = block.shape
    grouped = block.reshape(channels // PER, PER, row_count, col_count)
    return jnp.transpose(grouped, (3, 1, 0, 2)).reshape(col_count, channels * row_count)


def passed(value, axis, by):
    peers = lax.axis_size(axis)
    return lax.ppermute(value, axis, [(i, (i + by) % peers) for i in range(peers)])


def per_device(left_feats, right_feats, w_first, w_second, w_out):
    channels, row_count, col_count = left_feats.shape
    slots = lax.axis_size("grp")
    me = lax.axis_index("grp")
    cols = col_count // slots
    left, right = lax.optimization_barrier((by_column(left_feats), by_column(right_feats)))
    behind = HALO + SPREAD
    ahead = passed(
        jnp.concatenate([right[col_count - behind :], left[col_count - HALO :]], axis=0), "lon", 1
    )
    after = passed(jnp.concatenate([right[:HALO], left[:HALO]], axis=0), "lon", -1)
    left_wide = jnp.concatenate([ahead[behind:], left, after[HALO:]], axis=0)
    right_wide = jnp.concatenate([ahead[:behind], right, after[:HALO]], axis=0)
    windows = jnp.stack(
        [
            jnp.concatenate(
                [
                    left_wide[j * cols : j * cols + cols + 2 * HALO],
                    right_wide[j * cols : j * cols + cols + 2 * HALO + SPREAD],
                ],
                axis=0,
            )
            for j in range(slots)
        ]
    )
    feats = lax.all_to_all(windows, "grp", split_axis=0, concat_axis=0, tiled=True)
    order = jnp.arange(slots, dtype=jnp.int32)
    t1, t2, t3 = banded_weights(order, w_first, w_second, w_out, slots)
    part = aggregate(feats, t1, t2, t3, slots, cols)[:, :ROWS]
    share = row_count // slots
    split = part.reshape(cols, slots, share)
    rows = [lax.dynamic_index_in_dim(split, me, 1, keepdims=False)]
    for by in range(1, slots):
        target = (me + by) % slots
        rows.append(passed(lax.dynamic_index_in_dim(split, target, 1, keepdims=False), "grp", by))
    gathered = jnp.concatenate(rows, axis=0).reshape(slots, cols, share)
    placed = jnp.zeros_like(gathered)
    for by in range(slots):
        placed = lax.dynamic_update_index_in_dim(placed, gathered[by], (me - by) % slots, 0)
    return placed.reshape(col_count, share).T


def solution(mesh):
    placed = (P("grp", "pairs", "lon"), P("grp", "pairs", "lon"), P(), P(), P())
    return jax.shard_map(
        per_device,
        mesh=mesh,
        in_specs=placed,
        out_specs=P(("pairs", "grp"), "lon"),
        check_vma=False,
    )
```

```python
import functools

import jax
import jax.numpy as jnp
from jax import lax
from jax.experimental import pallas as pl
from jax.experimental.pallas import tpu as pltpu
from jax.sharding import PartitionSpec as P

C = 320
G = 40
CH = 32
DISP = 48
PER = C // G
ROWS = 16
HALF = ROWS // 2
LANE = 128
HALO = 4
SPREAD = DISP - 1
PARTS = 2
SHARE = G * ROWS // PARTS
WHOLE = SHARE // LANE * LANE
REST = SHARE - WHOLE
DEPTH = 3 * WHOLE + 4 * REST
FIRST_OUT = ROWS * CH
PART = FIRST_OUT // 2
CAP = 12.0


def weights_kernel(
    order_ref, w1_ref, w2_ref, w3_ref, t1_hbm, t2_hbm, t3_hbm, t1_ref, t2_ref, t3_ref, v1, sems, *, slots
):
    here = G // slots
    quarters = LANE // CH
    for tap in range(27):
        w1 = w1_ref[tap].astype(jnp.float32)
        v1[tap, :, :] = jnp.transpose(jnp.concatenate([w1] * quarters, axis=0))
    row16 = lax.broadcasted_iota(jnp.int32, (ROWS, LANE), 0)
    quarter = lax.broadcasted_iota(jnp.int32, (ROWS, LANE), 1) // CH
    masks = []
    for q in range(FIRST_OUT // LANE):
        at = quarters * q + quarter
        out_row = 2 * (at % HALF) + at // HALF
        masks.append(
            [jnp.where(row16 == out_row + kh - 1, 1.0, 0.0).astype(jnp.bfloat16) for kh in range(3)]
        )
    per_part = slots // PARTS
    for part in range(PARTS):
        for kw in range(3):

            def one_tap(t, carry):
                e, slot = t // per_part, t % per_part
                tap = (2 - e) * 9 + kw
                group = order_ref[part * per_part + slot] * here
                for i in range(here):
                    rows = []
                    for kh in range(3):
                        row = v1[tap + 3 * kh, pl.ds(group + i, 1), :]
                        rows.append(jnp.broadcast_to(row, (ROWS, LANE)).astype(jnp.bfloat16))
                    at = (slot * here + i) * ROWS
                    start = jnp.where(at < WHOLE, e * WHOLE + at, 3 * WHOLE + e * REST + at - WHOLE)
                    start = pl.multiple_of(start, ROWS)
                    for q in range(FIRST_OUT // LANE):
                        value = (
                            masks[q][0] * rows[0] + masks[q][1] * rows[1] + masks[q][2] * rows[2]
                        )
                        t1_ref[part, kw, pl.ds(start, ROWS), q * LANE : (q + 1) * LANE] = value
                return carry

            lax.fori_loop(0, 3 * per_part, one_tap, 0)
            t1_ref[part, kw, DEPTH - REST :, :] = jnp.zeros((REST, FIRST_OUT), jnp.bfloat16)
        pltpu.make_async_copy(t1_ref.at[part], t1_hbm.at[part], sems.at[part]).start()

    lane32 = lax.broadcasted_iota(jnp.int32, (CH, LANE), 1) // CH
    for kw in range(3):
        for e in range(3):
            tap = (2 - e) * 9 + kw
            v2 = [
                jnp.transpose(
                    jnp.concatenate([w2_ref[tap + 3 * kh].astype(jnp.float32)] * quarters, axis=0)
                )
                for kh in range(3)
            ]
            for hi in range(HALF):
                for q in range(PART // LANE):
                    value = jnp.zeros((CH, LANE), jnp.float32)
                    for kh in range(3):
                        if quarters * q <= hi - kh + 1 < quarters * (q + 1):
                            value = jnp.where(quarters * q + lane32 == hi - kh + 1, v2[kh], value)
                    start = e * PART + hi * CH
                    t2_ref[kw, start : start + CH, q * LANE : (q + 1) * LANE] = value.astype(
                        jnp.bfloat16
                    )
    pltpu.make_async_copy(t2_ref, t2_hbm, sems.at[3]).start()

    out_lane = lax.broadcasted_iota(jnp.int32, (CH, LANE), 1)
    for kw in range(3):
        v3 = []
        for kh in range(3):
            value = jnp.zeros((CH, LANE), jnp.float32)
            for e in range(3):
                tap = (2 - e) * 9 + 3 * kh + kw
                column = jnp.broadcast_to(w3_ref[:, tap : tap + 1], (CH, LANE))
                value = jnp.where(out_lane // ROWS == e, column, value)
            v3.append(value)
        for at in range(ROWS):
            hi = 2 * (at % HALF) + at // HALF
            value = jnp.zeros((CH, LANE), jnp.float32)
            for kh in range(3):
                value = jnp.where(out_lane % ROWS == hi - kh + 1, v3[kh], value)
            t3_ref[kw, at * CH : (at + 1) * CH, :] = value.astype(jnp.bfloat16)
    pltpu.make_async_copy(t3_ref, t3_hbm, sems.at[4]).start()
    for part in range(PARTS):
        pltpu.make_async_copy(t1_ref.at[part], t1_hbm.at[part], sems.at[part]).wait()
    pltpu.make_async_copy(t2_ref, t2_hbm, sems.at[3]).wait()
    pltpu.make_async_copy(t3_ref, t3_hbm, sems.at[4]).wait()


def banded_weights(order, w_first, w_second, w_out, slots):
    w1 = jnp.transpose(w_first, (2, 3, 4, 0, 1)).reshape(27, CH, G)
    w2 = jnp.transpose(w_second, (2, 3, 4, 0, 1)).reshape(27, CH, CH)
    w3 = w_out.reshape(CH, 27).astype(jnp.float32)
    whole = pl.BlockSpec(memory_space=pltpu.VMEM)
    far = pl.BlockSpec(memory_space=pltpu.HBM)
    shapes = [
        (PARTS, 3, DEPTH, FIRST_OUT),
        (3, 3 * PART, PART),
        (3, FIRST_OUT, LANE),
    ]
    return pl.pallas_call(
        functools.partial(weights_kernel, slots=slots),
        out_shape=tuple(jax.ShapeDtypeStruct(shape, jnp.bfloat16) for shape in shapes),
        in_specs=[pl.BlockSpec(memory_space=pltpu.SMEM), whole, whole, whole],
        out_specs=[far, far, far],
        scratch_shapes=[pltpu.VMEM(shape, jnp.bfloat16) for shape in shapes]
        + [pltpu.VMEM((27, G, LANE), jnp.float32), pltpu.SemaphoreType.DMA((5,))],
        compiler_params=pltpu.CompilerParams(vmem_limit_bytes=59 << 20),
        cost_estimate=pl.CostEstimate(flops=9_000_000, bytes_accessed=8_000_000, transcendentals=0),
        name="banded_weights",
    )(order, w1, w2, w3)


def cost_cells(feats, left, right, cells, cost_pad, slots, cols):
    span = G // slots * ROWS
    cost_cols = cols + 2 * HALO
    blocks = WHOLE // LANE
    for k in range(PER):
        pieces = [ref[:, k * span : (k + 1) * span].astype(jnp.float32) for ref in feats]
        pieces.append(jnp.zeros((pieces[0].shape[0], LANE - REST), jnp.float32))
        joined = jnp.concatenate(pieces, axis=1)
        for j in range(blocks + 1):
            tile = joined[:, j * LANE : (j + 1) * LANE]
            left[k * (blocks + 1) + j, :, :] = tile[:cost_cols]
            right[k * (blocks + 1) + j, :, :] = tile[cost_cols:]
    cost_pad[...] = jnp.zeros_like(cost_pad)

    def cost_column(w, carry):
        base = pl.multiple_of(w * DISP, DISP)
        for j in range(blocks + 1):
            total = None
            for k in range(PER):
                at = k * (blocks + 1) + j
                l_row = jnp.broadcast_to(left[at, pl.ds(w, 1), :], (DISP, LANE))
                term = l_row * right[at, pl.ds(w, DISP), :]
                total = term if total is None else total + term
            total = (total * (1.0 / PER)).astype(jnp.bfloat16)
            wide = total.astype(jnp.float32)
            cost_pad[j, 8 : 8 + DISP, :] = wide
            moved = [cost_pad[j, 7 : 7 + DISP, :], wide, cost_pad[j, 9 : 9 + DISP, :]]
            if j < blocks:
                for e in range(3):
                    lanes = e * WHOLE + j * LANE
                    cells[pl.ds(base, DISP), lanes : lanes + LANE] = moved[e].astype(jnp.bfloat16)
            else:
                pair = moved[0] + pltpu.roll(moved[1], REST, 1)
                lanes = 3 * WHOLE
                cells[pl.ds(base, DISP), lanes : lanes + LANE] = pair.astype(jnp.bfloat16)
                lanes += LANE
                cells[pl.ds(base, DISP), lanes : lanes + LANE] = moved[2].astype(jnp.bfloat16)
        return carry

    lax.fori_loop(0, cost_cols, cost_column, 0)


def first_kernel(*refs, slots, cols):
    feats = refs[: slots // PARTS]
    t1_hbm, acc_hbm, t1_ref, left, right, cells, cost_pad, acc, sems = refs[slots // PARTS :]
    fetches = [
        pltpu.make_async_copy(t1_hbm.at[0, kw], t1_ref.at[kw], sems.at[kw]) for kw in range(3)
    ]
    for fetch in fetches:
        fetch.start()
    cost_cells(feats, left, right, cells, cost_pad, slots, cols)
    half = (cols + 6) // 2
    for part in range(2):
        for kw in range(3):
            if part == 0:
                fetches[kw].wait()
            start = (part * half + kw) * DISP
            term = jnp.dot(
                cells[start : start + half * DISP, :], t1_ref[kw], preferred_element_type=jnp.float32
            )
            if kw == 0:
                acc[part, :, :] = term
            else:
                acc[part, :, :] += term
        pltpu.make_async_copy(acc.at[part], acc_hbm.at[part], sems.at[3 + part]).start()
    for part in range(2):
        pltpu.make_async_copy(acc.at[part], acc_hbm.at[part], sems.at[3 + part]).wait()


def main_kernel(*refs, slots, cols):
    feats = refs[: slots // PARTS]
    (
        t1_hbm, t2_hbm, t3_hbm, acc_hbm, out_ref,
        t1_ref, t2_ref, t3_ref, left, right, cells, cost_pad, acc, first, first_pad, second,
        score_pad, out_pad, sems,
    ) = refs[slots // PARTS :]
    fetches = [
        pltpu.make_async_copy(t1_hbm.at[1, kw], t1_ref.at[kw], sems.at[kw]) for kw in range(3)
    ]
    fetches += [
        pltpu.make_async_copy(acc_hbm, acc, sems.at[3]),
        pltpu.make_async_copy(t2_hbm, t2_ref, sems.at[4]),
        pltpu.make_async_copy(t3_hbm, t3_ref, sems.at[5]),
    ]
    for fetch in fetches:
        fetch.start()
    cost_cells(feats, left, right, cells, cost_pad, slots, cols)
    first_pad[...] = jnp.zeros_like(first_pad)
    fetches[3].wait()

    half1 = (cols + 6) // 2
    for part in range(2):
        for kw in range(3):
            if part == 0:
                fetches[kw].wait()
            start = (part * half1 + kw) * DISP
            acc[part, :, :] += jnp.dot(
                cells[start : start + half1 * DISP, :], t1_ref[kw], preferred_element_type=jnp.float32
            )

        def column(w, carry):
            local = pl.multiple_of(w * DISP, DISP)
            base = pl.multiple_of((part * half1 + w) * DISP, DISP)
            for q in range(FIRST_OUT // LANE):
                value = acc[part, pl.ds(local, DISP), q * LANE : (q + 1) * LANE]
                value = jnp.maximum(value, 0.0).astype(jnp.bfloat16)
                first_pad[q, 8 : 8 + DISP, :] = value.astype(jnp.float32)
                for e in range(3):
                    lanes = (q // 2) * 3 * PART + e * PART + (q % 2) * LANE
                    if e == 1:
                        moved = value
                    else:
                        moved = first_pad[q, 6 + 2 * e : 6 + 2 * e + DISP, :].astype(jnp.bfloat16)
                    first[pl.ds(base, DISP), lanes : lanes + LANE] = moved
            return carry

        lax.fori_loop(0, half1, column, 0)
    fetches[4].wait()

    half2 = (cols + 2) // 2

    def second_half(part, carry):
        out_at = pl.multiple_of(part * half2 * DISP, DISP)
        for p in range(2):
            lanes = p * 3 * PART
            total = None
            for kw in range(3):
                start = pl.multiple_of((part * half2 + 2 * kw) * DISP, DISP)
                term = jnp.dot(
                    first[pl.ds(start, half2 * DISP), lanes : lanes + 3 * PART],
                    t2_ref[kw],
                    preferred_element_type=jnp.float32,
                )
                total = term if total is None else total + term
            start = pl.multiple_of((part * half2 + 2) * DISP, DISP)
            kept = first[pl.ds(start, half2 * DISP), lanes + PART : lanes + 2 * PART]
            total = jnp.maximum(total + kept.astype(jnp.float32), 0.0).astype(jnp.bfloat16)
            second[pl.ds(out_at, half2 * DISP), p * PART : (p + 1) * PART] = total
        return carry

    lax.fori_loop(0, 2, second_half, 0)
    fetches[5].wait()

    total = None
    for kw in range(3):
        term = jnp.dot(
            second[kw * DISP : (kw + cols) * DISP, :], t3_ref[kw], preferred_element_type=jnp.float32
        )
        total = term if total is None else total + term
    score_pad[8 : 8 + cols * DISP, :] = total
    row = lax.broadcasted_iota(jnp.int32, (DISP, LANE), 0)
    level = ((DISP - 1) - row).astype(jnp.float32)

    def score_column(w, carry):
        base = pl.multiple_of(8 + w * DISP, 8)
        score = jnp.where(row == 0, 0.0, score_pad[pl.ds(base - 1, DISP), :])
        score = score + pltpu.roll(score_pad[pl.ds(base, DISP), :], LANE - ROWS, 1)
        later = jnp.where(row == DISP - 1, 0.0, score_pad[pl.ds(base + 1, DISP), :])
        score = score + pltpu.roll(later, LANE - 2 * ROWS, 1)
        weights = jnp.exp(CAP * jnp.tanh(score / CAP))
        bottom = jnp.sum(weights, axis=0, keepdims=True)
        top = jnp.sum(weights * level, axis=0, keepdims=True)
        out_pad[pl.ds(w, 1), :] = top / bottom / DISP
        return carry

    out_pad[...] = jnp.zeros_like(out_pad)
    score_pad[:8, :] = jnp.zeros((8, LANE), jnp.float32)
    score_pad[8 + cols * DISP :, :] = jnp.zeros((8, LANE), jnp.float32)
    lax.fori_loop(0, cols, score_column, 0, unroll=4)
    out_ref[...] = jnp.transpose(out_pad[...])[:ROWS]


def scratch(cols):
    cost_cols = cols + 2 * HALO
    tiles = PER * (WHOLE // LANE + 1)
    return [
        pltpu.VMEM((tiles, cost_cols, LANE), jnp.float32),
        pltpu.VMEM((tiles, cost_cols + SPREAD, LANE), jnp.float32),
        pltpu.VMEM((cost_cols * DISP, DEPTH), jnp.bfloat16),
        pltpu.VMEM((WHOLE // LANE + 1, DISP + 16, LANE), jnp.float32),
        pltpu.VMEM((2, (cols + 6) // 2 * DISP, FIRST_OUT), jnp.float32),
    ]


def first_part(feats, t1, slots, cols):
    whole = pl.BlockSpec(memory_space=pltpu.VMEM)
    far = pl.BlockSpec(memory_space=pltpu.HBM)
    return pl.pallas_call(
        functools.partial(first_kernel, slots=slots, cols=cols),
        out_shape=jax.ShapeDtypeStruct((2, (cols + 6) // 2 * DISP, FIRST_OUT), jnp.float32),
        in_specs=[whole] * len(feats) + [far],
        out_specs=far,
        scratch_shapes=[pltpu.VMEM((3, DEPTH, FIRST_OUT), jnp.bfloat16)]
        + scratch(cols)
        + [pltpu.SemaphoreType.DMA((5,))],
        compiler_params=pltpu.CompilerParams(vmem_limit_bytes=57 << 20),
        cost_estimate=pl.CostEstimate(
            flops=7_000_000_000, bytes_accessed=6_000_000, transcendentals=0
        ),
        name="first_part",
    )(*feats, t1)


def aggregate(feats, t1, t2, t3, acc, slots, cols):
    whole = pl.BlockSpec(memory_space=pltpu.VMEM)
    far = pl.BlockSpec(memory_space=pltpu.HBM)
    return pl.pallas_call(
        functools.partial(main_kernel, slots=slots, cols=cols),
        out_shape=jax.ShapeDtypeStruct((ROWS, LANE), jnp.float32),
        in_specs=[whole] * len(feats) + [far] * 4,
        out_specs=whole,
        scratch_shapes=[
            pltpu.VMEM((3, DEPTH, FIRST_OUT), jnp.bfloat16),
            pltpu.VMEM((3, 3 * PART, PART), jnp.bfloat16),
            pltpu.VMEM((3, FIRST_OUT, LANE), jnp.bfloat16),
        ]
        + scratch(cols)
        + [
            pltpu.VMEM(((cols + 6) * DISP, 3 * FIRST_OUT), jnp.bfloat16),
            pltpu.VMEM((FIRST_OUT // LANE, DISP + 16, LANE), jnp.float32),
            pltpu.VMEM(((cols + 2) * DISP, FIRST_OUT), jnp.bfloat16),
            pltpu.VMEM((cols * DISP + 16, LANE), jnp.float32),
            pltpu.VMEM((LANE, LANE), jnp.float32),
            pltpu.SemaphoreType.DMA((6,)),
        ],
        compiler_params=pltpu.CompilerParams(vmem_limit_bytes=57 << 20),
        name="aggregate",
    )(*feats, t1, t2, t3, acc)


def by_column(block):
    channels, row_count, col_count = block.shape
    grouped = block.reshape(channels // PER, PER, row_count, col_count)
    return jnp.transpose(grouped, (3, 1, 0, 2)).reshape(col_count, channels * row_count)


def passed(value, axis, by):
    peers = lax.axis_size(axis)
    return lax.ppermute(value, axis, [(i, (i + by) % peers) for i in range(peers)])


def per_device(left_feats, right_feats, w_first, w_second, w_out):
    channels, row_count, col_count = left_feats.shape
    slots = lax.axis_size("grp")
    me = lax.axis_index("grp")
    cols = col_count // slots
    left, right = lax.optimization_barrier((by_column(left_feats), by_column(right_feats)))
    behind = HALO + SPREAD
    ahead = passed(
        jnp.concatenate([right[col_count - behind :], left[col_count - HALO :]], axis=0), "lon", 1
    )
    after = passed(jnp.concatenate([right[:HALO], left[:HALO]], axis=0), "lon", -1)
    order = jnp.arange(slots, dtype=jnp.int32) ^ me
    t1, t2, t3 = banded_weights(order, w_first, w_second, w_out, slots)
    left_wide = jnp.concatenate([ahead[behind:], left, after[HALO:]], axis=0)
    right_wide = jnp.concatenate([ahead[:behind], right, after[:HALO]], axis=0)
    def window(target):
        start = target * cols
        return jnp.concatenate(
            [
                lax.dynamic_slice_in_dim(left_wide, start, cols + 2 * HALO, 0),
                lax.dynamic_slice_in_dim(right_wide, start, cols + 2 * HALO + SPREAD, 0),
            ],
            axis=0,
        )

    feats = [window(me)]
    for t in range(1, slots):
        feats.append(lax.ppermute(window(me ^ t), "grp", [(i, i ^ t) for i in range(slots)]))
    near = slots // PARTS
    acc = first_part(feats[:near], t1, slots, cols)
    result = aggregate(feats[near:], t1, t2, t3, acc, slots, cols)
    share = row_count // slots

    def rows_of(target):
        return lax.dynamic_slice(result, (target * share, 0), (share, cols))

    pieces = [rows_of(me)]
    for t in range(1, slots):
        pieces.append(lax.ppermute(rows_of(me ^ t), "grp", [(i, i ^ t) for i in range(slots)]))
    bit = 1
    while bit < slots:
        swap = (me & bit) > 0
        pieces = [jnp.where(swap, pieces[t ^ bit], pieces[t]) for t in range(slots)]
        bit *= 2
    return jnp.concatenate(pieces, axis=1)


def solution(mesh):
    placed = (P("grp", "pairs", "lon"), P("grp", "pairs", "lon"), P(), P(), P())
    return jax.shard_map(
        per_device,
        mesh=mesh,
        in_specs=placed,
        out_specs=P(("pairs", "grp"), "lon"),
        check_vma=False,
    )
```

```python
import functools

import jax
import jax.numpy as jnp
from jax import lax
from jax.experimental import pallas as pl
from jax.experimental.pallas import tpu as pltpu
from jax.sharding import PartitionSpec as P

C = 320
G = 40
CH = 32
DISP = 48
PER = C // G
ROWS = 16
HALF = ROWS // 2
LANE = 128
HALO = 4
SPREAD = DISP - 1
PARTS = 2
SHARE = G * ROWS // PARTS
WHOLE = SHARE // LANE * LANE
REST = SHARE - WHOLE
DEPTH = 3 * WHOLE + 4 * REST
FIRST_OUT = ROWS * CH
PART = FIRST_OUT // 2
CAP = 12.0


def weights_kernel(
    w1_ref, w2_ref, w3_ref, t1_hbm, t2_hbm, t3_hbm, t1_ref, t2_ref, t3_ref, v1, v3_ref, sems, *, slots
):
    here = G // slots
    me = lax.axis_index("grp")
    quarters = LANE // CH
    for tap in range(27):
        w1 = w1_ref[tap].astype(jnp.float32)
        v1[tap, :, :] = jnp.transpose(jnp.concatenate([w1] * quarters, axis=0))
    row16 = lax.broadcasted_iota(jnp.int32, (ROWS, LANE), 0)
    quarter = lax.broadcasted_iota(jnp.int32, (ROWS, LANE), 1) // CH
    masks = []
    for q in range(FIRST_OUT // LANE):
        at = quarters * q + quarter
        out_row = 2 * (at % HALF) + at // HALF
        masks.append(
            [jnp.where(row16 == out_row + kh - 1, 1.0, 0.0).astype(jnp.bfloat16) for kh in range(3)]
        )
    per_part = slots // PARTS
    for part in range(PARTS):
        for kw in range(3):

            def one_tap(t, carry):
                e, slot = t // per_part, t % per_part
                tap = (2 - e) * 9 + kw
                group = (me ^ (part * per_part + slot)) * here
                for i in range(here):
                    rows = []
                    for kh in range(3):
                        row = v1[tap + 3 * kh, pl.ds(group + i, 1), :]
                        rows.append(jnp.broadcast_to(row, (ROWS, LANE)).astype(jnp.bfloat16))
                    at = (slot * here + i) * ROWS
                    start = jnp.where(at < WHOLE, e * WHOLE + at, 3 * WHOLE + e * REST + at - WHOLE)
                    start = pl.multiple_of(start, ROWS)
                    for q in range(FIRST_OUT // LANE):
                        value = (
                            masks[q][0] * rows[0] + masks[q][1] * rows[1] + masks[q][2] * rows[2]
                        )
                        t1_ref[part, kw, pl.ds(start, ROWS), q * LANE : (q + 1) * LANE] = value
                return carry

            lax.fori_loop(0, 3 * per_part, one_tap, 0)
            t1_ref[part, kw, DEPTH - REST :, :] = jnp.zeros((REST, FIRST_OUT), jnp.bfloat16)
        pltpu.make_async_copy(t1_ref.at[part], t1_hbm.at[part], sems.at[part]).start()

    lane32 = lax.broadcasted_iota(jnp.int32, (CH, LANE), 1) // CH
    for kw in range(3):
        for e in range(3):
            tap = (2 - e) * 9 + kw
            v2 = [
                jnp.transpose(
                    jnp.concatenate([w2_ref[tap + 3 * kh].astype(jnp.float32)] * quarters, axis=0)
                )
                for kh in range(3)
            ]
            for hi in range(HALF):
                for q in range(PART // LANE):
                    value = jnp.zeros((CH, LANE), jnp.float32)
                    for kh in range(3):
                        if quarters * q <= hi - kh + 1 < quarters * (q + 1):
                            value = jnp.where(quarters * q + lane32 == hi - kh + 1, v2[kh], value)
                    start = e * PART + hi * CH
                    t2_ref[kw, start : start + CH, q * LANE : (q + 1) * LANE] = value.astype(
                        jnp.bfloat16
                    )
    pltpu.make_async_copy(t2_ref, t2_hbm, sems.at[3]).start()

    v3_ref[...] = jnp.zeros_like(v3_ref)
    for i in range(9):
        v3_ref[3 * i : 3 * i + 3, :CH] = w3_ref[i].astype(jnp.float32)
    taps = jnp.transpose(v3_ref[...])[:CH]
    out_lane = lax.broadcasted_iota(jnp.int32, (CH, LANE), 1)
    for kw in range(3):
        v3 = []
        for kh in range(3):
            value = jnp.zeros((CH, LANE), jnp.float32)
            for e in range(3):
                tap = (2 - e) * 9 + 3 * kh + kw
                column = jnp.broadcast_to(taps[:, tap : tap + 1], (CH, LANE))
                value = jnp.where(out_lane // ROWS == e, column, value)
            v3.append(value)
        for at in range(ROWS):
            hi = 2 * (at % HALF) + at // HALF
            value = jnp.zeros((CH, LANE), jnp.float32)
            for kh in range(3):
                value = jnp.where(out_lane % ROWS == hi - kh + 1, v3[kh], value)
            t3_ref[kw, at * CH : (at + 1) * CH, :] = value.astype(jnp.bfloat16)
    pltpu.make_async_copy(t3_ref, t3_hbm, sems.at[4]).start()
    for part in range(PARTS):
        pltpu.make_async_copy(t1_ref.at[part], t1_hbm.at[part], sems.at[part]).wait()
    pltpu.make_async_copy(t2_ref, t2_hbm, sems.at[3]).wait()
    pltpu.make_async_copy(t3_ref, t3_hbm, sems.at[4]).wait()


def banded_weights(w_first, w_second, w_out, slots):
    w1 = jnp.transpose(w_first, (2, 3, 4, 0, 1)).reshape(27, CH, G)
    w2 = jnp.transpose(w_second, (2, 3, 4, 0, 1)).reshape(27, CH, CH)
    w3 = jnp.transpose(w_out, (0, 2, 3, 4, 1)).reshape(9, 3, CH)
    whole = pl.BlockSpec(memory_space=pltpu.VMEM)
    far = pl.BlockSpec(memory_space=pltpu.HBM)
    shapes = [
        (PARTS, 3, DEPTH, FIRST_OUT),
        (3, 3 * PART, PART),
        (3, FIRST_OUT, LANE),
    ]
    return pl.pallas_call(
        functools.partial(weights_kernel, slots=slots),
        out_shape=tuple(jax.ShapeDtypeStruct(shape, jnp.bfloat16) for shape in shapes),
        in_specs=[whole, whole, whole],
        out_specs=[far, far, far],
        scratch_shapes=[pltpu.VMEM(shape, jnp.bfloat16) for shape in shapes]
        + [
            pltpu.VMEM((27, G, LANE), jnp.float32),
            pltpu.VMEM((LANE, LANE), jnp.float32),
            pltpu.SemaphoreType.DMA((5,)),
        ],
        compiler_params=pltpu.CompilerParams(vmem_limit_bytes=59 << 20),
        cost_estimate=pl.CostEstimate(flops=9_000_000, bytes_accessed=8_000_000, transcendentals=0),
        name="banded_weights",
    )(w1, w2, w3)


def cost_cells(feats, left, right, cells, cost_pad, slots, cols):
    span = G // slots * ROWS
    cost_cols = cols + 2 * HALO
    blocks = WHOLE // LANE
    for k in range(PER):
        pieces = [ref[:, k * span : (k + 1) * span].astype(jnp.float32) for ref in feats]
        pieces.append(jnp.zeros((pieces[0].shape[0], LANE - REST), jnp.float32))
        joined = jnp.concatenate(pieces, axis=1)
        for j in range(blocks + 1):
            tile = joined[:, j * LANE : (j + 1) * LANE]
            left[k * (blocks + 1) + j, :, :] = tile[:cost_cols]
            right[k * (blocks + 1) + j, :, :] = tile[cost_cols:]
    cost_pad[...] = jnp.zeros_like(cost_pad)

    def cost_column(w, carry):
        base = pl.multiple_of(w * DISP, DISP)
        for j in range(blocks + 1):
            total = None
            for k in range(PER):
                at = k * (blocks + 1) + j
                l_row = jnp.broadcast_to(left[at, pl.ds(w, 1), :], (DISP, LANE))
                term = l_row * right[at, pl.ds(w, DISP), :]
                total = term if total is None else total + term
            total = (total * (1.0 / PER)).astype(jnp.bfloat16)
            wide = total.astype(jnp.float32)
            cost_pad[j, 8 : 8 + DISP, :] = wide
            moved = [cost_pad[j, 7 : 7 + DISP, :], wide, cost_pad[j, 9 : 9 + DISP, :]]
            if j < blocks:
                for e in range(3):
                    lanes = e * WHOLE + j * LANE
                    cells[pl.ds(base, DISP), lanes : lanes + LANE] = moved[e].astype(jnp.bfloat16)
            else:
                pair = moved[0] + pltpu.roll(moved[1], REST, 1)
                lanes = 3 * WHOLE
                cells[pl.ds(base, DISP), lanes : lanes + LANE] = pair.astype(jnp.bfloat16)
                lanes += LANE
                cells[pl.ds(base, DISP), lanes : lanes + LANE] = moved[2].astype(jnp.bfloat16)
        return carry

    lax.fori_loop(0, cost_cols, cost_column, 0, unroll=2)


def first_kernel(*refs, slots, cols):
    feats = refs[: slots // PARTS]
    t1_hbm, acc_hbm, t1_ref, left, right, cells, cost_pad, acc, sems = refs[slots // PARTS :]
    fetches = [
        pltpu.make_async_copy(t1_hbm.at[0, kw], t1_ref.at[kw], sems.at[kw]) for kw in range(3)
    ]
    for fetch in fetches:
        fetch.start()
    cost_cells(feats, left, right, cells, cost_pad, slots, cols)
    half = (cols + 6) // 2
    for part in range(2):
        for kw in range(3):
            if part == 0:
                fetches[kw].wait()
            start = (part * half + kw) * DISP
            term = jnp.dot(
                cells[start : start + half * DISP, :], t1_ref[kw], preferred_element_type=jnp.float32
            )
            if kw == 0:
                acc[part, :, :] = term
            else:
                acc[part, :, :] += term
        pltpu.make_async_copy(acc.at[part], acc_hbm.at[part], sems.at[3 + part]).start()
    for part in range(2):
        pltpu.make_async_copy(acc.at[part], acc_hbm.at[part], sems.at[3 + part]).wait()


def main_kernel(*refs, slots, cols):
    feats = refs[: slots // PARTS]
    t1_hbm, t2_hbm, t3_hbm, acc_hbm = refs[slots // PARTS : slots // PARTS + 4]
    outs = refs[slots // PARTS + 4 : slots // PARTS + 4 + slots]
    (
        t1_ref, t2_ref, t3_ref, left, right, cells, cost_pad, acc, first, first_pad, second,
        score_pad, out_pad, sems,
    ) = refs[slots // PARTS + 4 + slots :]
    fetches = [
        pltpu.make_async_copy(t1_hbm.at[1, kw], t1_ref.at[kw], sems.at[kw]) for kw in range(3)
    ]
    fetches += [
        pltpu.make_async_copy(acc_hbm, acc, sems.at[3]),
        pltpu.make_async_copy(t2_hbm, t2_ref, sems.at[4]),
        pltpu.make_async_copy(t3_hbm, t3_ref, sems.at[5]),
    ]
    for fetch in fetches:
        fetch.start()
    cost_cells(feats, left, right, cells, cost_pad, slots, cols)
    first_pad[...] = jnp.zeros_like(first_pad)
    fetches[3].wait()

    half1 = (cols + 6) // 2
    for part in range(2):
        for kw in range(3):
            if part == 0:
                fetches[kw].wait()
            start = (part * half1 + kw) * DISP
            acc[part, :, :] += jnp.dot(
                cells[start : start + half1 * DISP, :], t1_ref[kw], preferred_element_type=jnp.float32
            )

        def column(w, carry):
            local = pl.multiple_of(w * DISP, DISP)
            base = pl.multiple_of((part * half1 + w) * DISP, DISP)
            for q in range(FIRST_OUT // LANE):
                value = acc[part, pl.ds(local, DISP), q * LANE : (q + 1) * LANE]
                value = jnp.maximum(value, 0.0).astype(jnp.bfloat16)
                first_pad[q, 8 : 8 + DISP, :] = value.astype(jnp.float32)
                for e in range(3):
                    lanes = (q // 2) * 3 * PART + e * PART + (q % 2) * LANE
                    if e == 1:
                        moved = value
                    else:
                        moved = first_pad[q, 6 + 2 * e : 6 + 2 * e + DISP, :].astype(jnp.bfloat16)
                    first[pl.ds(base, DISP), lanes : lanes + LANE] = moved
            return carry

        lax.fori_loop(0, half1, column, 0)
    fetches[4].wait()

    half2 = (cols + 2) // 2

    def second_half(part, carry):
        out_at = pl.multiple_of(part * half2 * DISP, DISP)
        for p in range(2):
            lanes = p * 3 * PART
            total = None
            for kw in range(3):
                start = pl.multiple_of((part * half2 + 2 * kw) * DISP, DISP)
                term = jnp.dot(
                    first[pl.ds(start, half2 * DISP), lanes : lanes + 3 * PART],
                    t2_ref[kw],
                    preferred_element_type=jnp.float32,
                )
                total = term if total is None else total + term
            start = pl.multiple_of((part * half2 + 2) * DISP, DISP)
            kept = first[pl.ds(start, half2 * DISP), lanes + PART : lanes + 2 * PART]
            total = jnp.maximum(total + kept.astype(jnp.float32), 0.0).astype(jnp.bfloat16)
            second[pl.ds(out_at, half2 * DISP), p * PART : (p + 1) * PART] = total
        return carry

    lax.fori_loop(0, 2, second_half, 0)
    fetches[5].wait()

    total = None
    for kw in range(3):
        term = jnp.dot(
            second[kw * DISP : (kw + cols) * DISP, :], t3_ref[kw], preferred_element_type=jnp.float32
        )
        total = term if total is None else total + term
    score_pad[8 : 8 + cols * DISP, :] = total
    row = lax.broadcasted_iota(jnp.int32, (DISP, LANE), 0)
    level = ((DISP - 1) - row).astype(jnp.float32)

    def score_column(w, carry):
        base = pl.multiple_of(8 + w * DISP, 8)
        score = jnp.where(row == 0, 0.0, score_pad[pl.ds(base - 1, DISP), :])
        score = score + pltpu.roll(score_pad[pl.ds(base, DISP), :], LANE - ROWS, 1)
        later = jnp.where(row == DISP - 1, 0.0, score_pad[pl.ds(base + 1, DISP), :])
        score = score + pltpu.roll(later, LANE - 2 * ROWS, 1)
        weights = jnp.exp(CAP * jnp.tanh(score / CAP))
        bottom = jnp.sum(weights, axis=0, keepdims=True)
        top = jnp.sum(weights * level, axis=0, keepdims=True)
        out_pad[pl.ds(w, 1), :] = top / bottom / DISP
        return carry

    out_pad[...] = jnp.zeros_like(out_pad)
    score_pad[:8, :] = jnp.zeros((8, LANE), jnp.float32)
    score_pad[8 + cols * DISP :, :] = jnp.zeros((8, LANE), jnp.float32)
    lax.fori_loop(0, cols, score_column, 0, unroll=4)
    out_pad[...] = jnp.transpose(out_pad[...])
    me = lax.axis_index("grp")
    share = ROWS // slots
    for t in range(slots):
        outs[t][...] = out_pad[pl.ds((me ^ t) * share, share), :cols]


def scratch(cols):
    cost_cols = cols + 2 * HALO
    tiles = PER * (WHOLE // LANE + 1)
    return [
        pltpu.VMEM((tiles, cost_cols, LANE), jnp.float32),
        pltpu.VMEM((tiles, cost_cols + SPREAD, LANE), jnp.float32),
        pltpu.VMEM((cost_cols * DISP, DEPTH), jnp.bfloat16),
        pltpu.VMEM((WHOLE // LANE + 1, DISP + 16, LANE), jnp.float32),
        pltpu.VMEM((2, (cols + 6) // 2 * DISP, FIRST_OUT), jnp.float32),
    ]


def first_part(feats, t1, slots, cols):
    whole = pl.BlockSpec(memory_space=pltpu.VMEM)
    far = pl.BlockSpec(memory_space=pltpu.HBM)
    return pl.pallas_call(
        functools.partial(first_kernel, slots=slots, cols=cols),
        out_shape=jax.ShapeDtypeStruct((2, (cols + 6) // 2 * DISP, FIRST_OUT), jnp.float32),
        in_specs=[whole] * len(feats) + [far],
        out_specs=far,
        scratch_shapes=[pltpu.VMEM((3, DEPTH, FIRST_OUT), jnp.bfloat16)]
        + scratch(cols)
        + [pltpu.SemaphoreType.DMA((5,))],
        compiler_params=pltpu.CompilerParams(vmem_limit_bytes=46 << 20),
        cost_estimate=pl.CostEstimate(
            flops=7_000_000_000, bytes_accessed=6_000_000, transcendentals=0
        ),
        name="first_part",
    )(*feats, t1)


def aggregate(feats, t1, t2, t3, acc, slots, cols):
    whole = pl.BlockSpec(memory_space=pltpu.VMEM)
    far = pl.BlockSpec(memory_space=pltpu.HBM)
    return pl.pallas_call(
        functools.partial(main_kernel, slots=slots, cols=cols),
        out_shape=[jax.ShapeDtypeStruct((ROWS // slots, cols), jnp.float32)] * slots,
        in_specs=[whole] * len(feats) + [far] * 4,
        out_specs=[whole] * slots,
        scratch_shapes=[
            pltpu.VMEM((3, DEPTH, FIRST_OUT), jnp.bfloat16),
            pltpu.VMEM((3, 3 * PART, PART), jnp.bfloat16),
            pltpu.VMEM((3, FIRST_OUT, LANE), jnp.bfloat16),
        ]
        + scratch(cols)
        + [
            pltpu.VMEM(((cols + 6) * DISP, 3 * FIRST_OUT), jnp.bfloat16),
            pltpu.VMEM((FIRST_OUT // LANE, DISP + 16, LANE), jnp.float32),
            pltpu.VMEM(((cols + 2) * DISP, FIRST_OUT), jnp.bfloat16),
            pltpu.VMEM((cols * DISP + 16, LANE), jnp.float32),
            pltpu.VMEM((LANE, LANE), jnp.float32),
            pltpu.SemaphoreType.DMA((6,)),
        ],
        compiler_params=pltpu.CompilerParams(vmem_limit_bytes=46 << 20),
        name="aggregate",
    )(*feats, t1, t2, t3, acc)


def by_column(block):
    channels, row_count, col_count = block.shape
    grouped = block.reshape(channels // PER, PER, row_count, col_count)
    return jnp.transpose(grouped, (3, 1, 0, 2)).reshape(col_count, channels * row_count)


def passed(value, axis, by):
    peers = lax.axis_size(axis)
    return lax.ppermute(value, axis, [(i, (i + by) % peers) for i in range(peers)])


def per_device(left_feats, right_feats, w_first, w_second, w_out):
    channels, row_count, col_count = left_feats.shape
    slots = lax.axis_size("grp")
    me = lax.axis_index("grp")
    cols = col_count // slots
    left, right = lax.optimization_barrier((by_column(left_feats), by_column(right_feats)))
    behind = HALO + SPREAD
    ahead = passed(
        jnp.concatenate([right[col_count - behind :], left[col_count - HALO :]], axis=0), "lon", 1
    )
    after = passed(jnp.concatenate([right[:HALO], left[:HALO]], axis=0), "lon", -1)
    t1, t2, t3 = banded_weights(w_first, w_second, w_out, slots)
    left_wide = jnp.concatenate([ahead[behind:], left, after[HALO:]], axis=0)
    right_wide = jnp.concatenate([ahead[:behind], right, after[:HALO]], axis=0)
    def window(target):
        start = target * cols
        return jnp.concatenate(
            [
                lax.dynamic_slice_in_dim(left_wide, start, cols + 2 * HALO, 0),
                lax.dynamic_slice_in_dim(right_wide, start, cols + 2 * HALO + SPREAD, 0),
            ],
            axis=0,
        )

    feats = [window(me)]
    for t in range(1, slots):
        feats.append(lax.ppermute(window(me ^ t), "grp", [(i, i ^ t) for i in range(slots)]))
    near = slots // PARTS
    acc = first_part(feats[:near], t1, slots, cols)
    pieces = aggregate(feats[near:], t1, t2, t3, acc, slots, cols)
    out = jnp.zeros((row_count // slots, col_count), jnp.float32)
    for t in range(slots):
        piece = pieces[t]
        if t > 0:
            piece = lax.ppermute(piece, "grp", [(i, i ^ t) for i in range(slots)])
        out = lax.dynamic_update_slice_in_dim(out, piece, (me ^ t) * cols, 1)
    return out


def solution(mesh):
    placed = (P("grp", "pairs", "lon"), P("grp", "pairs", "lon"), P(), P(), P())
    return jax.shard_map(
        per_device,
        mesh=mesh,
        in_specs=placed,
        out_specs=P(("pairs", "grp"), "lon"),
        check_vma=False,
    )
```

```python
import functools

import jax
import jax.numpy as jnp
from jax import lax
from jax.experimental import pallas as pl
from jax.experimental.pallas import tpu as pltpu
from jax.sharding import PartitionSpec as P

C = 320
G = 40
CH = 32
DISP = 48
PER = C // G
ROWS = 16
HALF = ROWS // 2
LANE = 128
HALO = 4
SPREAD = DISP - 1
PARTS = 2
SHARE = G * ROWS // PARTS
WHOLE = SHARE // LANE * LANE
REST = SHARE - WHOLE
DEPTH = 3 * WHOLE + 4 * REST
FIRST_OUT = ROWS * CH
PART = FIRST_OUT // 2
CAP = 12.0


def weights_kernel(
    w1_ref, w2_ref, w3_ref, t1a_ref, t1b_ref, t2_ref, t3_ref, v1, v3_ref, *, slots
):
    here = G // slots
    me = lax.axis_index("grp")
    quarters = LANE // CH
    for tap in range(27):
        w1 = w1_ref[tap].astype(jnp.float32)
        v1[tap, :, :] = jnp.transpose(jnp.concatenate([w1] * quarters, axis=0))
    row16 = lax.broadcasted_iota(jnp.int32, (ROWS, LANE), 0)
    quarter = lax.broadcasted_iota(jnp.int32, (ROWS, LANE), 1) // CH
    masks = []
    for q in range(FIRST_OUT // LANE):
        at = quarters * q + quarter
        out_row = 2 * (at % HALF) + at // HALF
        masks.append(
            [jnp.where(row16 == out_row + kh - 1, 1.0, 0.0).astype(jnp.bfloat16) for kh in range(3)]
        )
    per_part = slots // PARTS
    for part, t1_ref in enumerate((t1a_ref, t1b_ref)):
        for kw in range(3):

            def one_tap(t, carry):
                e, slot = t // per_part, t % per_part
                tap = (2 - e) * 9 + kw
                group = (me ^ (part * per_part + slot)) * here
                for i in range(here):
                    rows = []
                    for kh in range(3):
                        row = v1[tap + 3 * kh, pl.ds(group + i, 1), :]
                        rows.append(jnp.broadcast_to(row, (ROWS, LANE)).astype(jnp.bfloat16))
                    at = (slot * here + i) * ROWS
                    start = jnp.where(at < WHOLE, e * WHOLE + at, 3 * WHOLE + e * REST + at - WHOLE)
                    start = pl.multiple_of(start, ROWS)
                    for q in range(FIRST_OUT // LANE):
                        value = (
                            masks[q][0] * rows[0] + masks[q][1] * rows[1] + masks[q][2] * rows[2]
                        )
                        t1_ref[kw, pl.ds(start, ROWS), q * LANE : (q + 1) * LANE] = value
                return carry

            lax.fori_loop(0, 3 * per_part, one_tap, 0)
            t1_ref[kw, DEPTH - REST :, :] = jnp.zeros((REST, FIRST_OUT), jnp.bfloat16)

    lane32 = lax.broadcasted_iota(jnp.int32, (CH, LANE), 1) // CH
    for kw in range(3):
        for e in range(3):
            tap = (2 - e) * 9 + kw
            v2 = [
                jnp.transpose(
                    jnp.concatenate([w2_ref[tap + 3 * kh].astype(jnp.float32)] * quarters, axis=0)
                )
                for kh in range(3)
            ]
            for hi in range(HALF):
                for q in range(PART // LANE):
                    value = jnp.zeros((CH, LANE), jnp.float32)
                    for kh in range(3):
                        if quarters * q <= hi - kh + 1 < quarters * (q + 1):
                            value = jnp.where(quarters * q + lane32 == hi - kh + 1, v2[kh], value)
                    start = e * PART + hi * CH
                    t2_ref[kw, start : start + CH, q * LANE : (q + 1) * LANE] = value.astype(
                        jnp.bfloat16
                    )

    v3_ref[...] = jnp.zeros_like(v3_ref)
    for i in range(9):
        v3_ref[3 * i : 3 * i + 3, :CH] = w3_ref[i].astype(jnp.float32)
    taps = jnp.transpose(v3_ref[...])[:CH]
    out_lane = lax.broadcasted_iota(jnp.int32, (CH, LANE), 1)
    for kw in range(3):
        v3 = []
        for kh in range(3):
            value = jnp.zeros((CH, LANE), jnp.float32)
            for e in range(3):
                tap = (2 - e) * 9 + 3 * kh + kw
                column = jnp.broadcast_to(taps[:, tap : tap + 1], (CH, LANE))
                value = jnp.where(out_lane // ROWS == e, column, value)
            v3.append(value)
        for at in range(ROWS):
            hi = 2 * (at % HALF) + at // HALF
            value = jnp.zeros((CH, LANE), jnp.float32)
            for kh in range(3):
                value = jnp.where(out_lane % ROWS == hi - kh + 1, v3[kh], value)
            t3_ref[kw, at * CH : (at + 1) * CH, :] = value.astype(jnp.bfloat16)


def banded_weights(w_first, w_second, w_out, slots):
    w1 = jnp.transpose(w_first, (2, 3, 4, 0, 1)).reshape(27, CH, G)
    w2 = jnp.transpose(w_second, (2, 3, 4, 0, 1)).reshape(27, CH, CH)
    w3 = jnp.transpose(w_out, (0, 2, 3, 4, 1)).reshape(9, 3, CH)
    whole = pl.BlockSpec(memory_space=pltpu.VMEM)
    shapes = [
        (3, DEPTH, FIRST_OUT),
        (3, DEPTH, FIRST_OUT),
        (3, 3 * PART, PART),
        (3, FIRST_OUT, LANE),
    ]
    return pl.pallas_call(
        functools.partial(weights_kernel, slots=slots),
        out_shape=tuple(jax.ShapeDtypeStruct(shape, jnp.bfloat16) for shape in shapes),
        in_specs=[whole, whole, whole],
        out_specs=[whole] * 4,
        scratch_shapes=[
            pltpu.VMEM((27, G, LANE), jnp.float32),
            pltpu.VMEM((LANE, LANE), jnp.float32),
        ],
        compiler_params=pltpu.CompilerParams(vmem_limit_bytes=8 << 20),
        cost_estimate=pl.CostEstimate(flops=9_000_000, bytes_accessed=8_000_000, transcendentals=0),
        name="banded_weights",
    )(w1, w2, w3)


def cost_cells(feats, left, right, cells, cost_pad, slots, cols):
    span = G // slots * ROWS
    cost_cols = cols + 2 * HALO
    blocks = WHOLE // LANE
    behind = HALO + SPREAD

    def joined(refs, k):
        pieces = [ref[:, k * span : (k + 1) * span].astype(jnp.float32) for ref in refs]
        pieces.append(jnp.zeros((pieces[0].shape[0], LANE - REST), jnp.float32))
        return jnp.concatenate(pieces, axis=1)

    for k in range(PER):
        inner, outer = joined(feats[0::2], k), joined(feats[1::2], k)
        for j in range(blocks + 1):
            at = k * (blocks + 1) + j
            mine = inner[:, j * LANE : (j + 1) * LANE]
            edge = outer[:, j * LANE : (j + 1) * LANE]
            right[at, :behind, :] = edge[:behind]
            right[at, behind : behind + cols, :] = mine[:cols]
            right[at, behind + cols :, :] = edge[behind : behind + HALO]
            left[at, :HALO, :] = edge[behind + HALO : behind + 2 * HALO]
            left[at, HALO : HALO + cols, :] = mine[cols:]
            left[at, HALO + cols :, :] = edge[behind + 2 * HALO :]
    cost_pad[...] = jnp.zeros_like(cost_pad)

    def cost_column(w, carry):
        base = pl.multiple_of(w * DISP, DISP)
        for j in range(blocks + 1):
            total = None
            for k in range(PER):
                at = k * (blocks + 1) + j
                l_row = jnp.broadcast_to(left[at, pl.ds(w, 1), :], (DISP, LANE))
                term = l_row * right[at, pl.ds(w, DISP), :]
                total = term if total is None else total + term
            total = (total * (1.0 / PER)).astype(jnp.bfloat16)
            wide = total.astype(jnp.float32)
            cost_pad[j, 8 : 8 + DISP, :] = wide
            moved = [cost_pad[j, 7 : 7 + DISP, :], wide, cost_pad[j, 9 : 9 + DISP, :]]
            if j < blocks:
                for e in range(3):
                    lanes = e * WHOLE + j * LANE
                    cells[pl.ds(base, DISP), lanes : lanes + LANE] = moved[e].astype(jnp.bfloat16)
            else:
                pair = moved[0] + pltpu.roll(moved[1], REST, 1)
                lanes = 3 * WHOLE
                cells[pl.ds(base, DISP), lanes : lanes + LANE] = pair.astype(jnp.bfloat16)
                lanes += LANE
                cells[pl.ds(base, DISP), lanes : lanes + LANE] = moved[2].astype(jnp.bfloat16)
        return carry

    lax.fori_loop(0, cost_cols, cost_column, 0, unroll=2)


def first_kernel(*refs, slots, cols):
    count = 2 * slots // PARTS
    t1_ref, acc, left, right, cells, cost_pad = refs[count:]
    cost_cells(refs[:count], left, right, cells, cost_pad, slots, cols)
    half = (cols + 6) // 2
    for part in range(2):
        total = None
        for kw in range(3):
            start = (part * half + kw) * DISP
            term = jnp.dot(
                cells[start : start + half * DISP, :], t1_ref[kw], preferred_element_type=jnp.float32
            )
            total = term if total is None else total + term
        acc[part, :, :] = total


def main_kernel(*refs, slots, cols):
    count = 2 * slots // PARTS
    t1_ref, t2_ref, t3_ref, acc_ref = refs[count : count + 4]
    outs = refs[count + 4 : count + 4 + slots]
    (
        left, right, cells, cost_pad, acc, first, first_pad, second, score_pad, out_pad,
    ) = refs[count + 4 + slots :]
    cost_cells(refs[:count], left, right, cells, cost_pad, slots, cols)
    first_pad[...] = jnp.zeros_like(first_pad)

    half1 = (cols + 6) // 2
    for part in range(2):
        total = acc_ref[part, :, :]
        for kw in range(3):
            start = (part * half1 + kw) * DISP
            total = total + jnp.dot(
                cells[start : start + half1 * DISP, :], t1_ref[kw], preferred_element_type=jnp.float32
            )
        acc[:, :] = total

        def column(w, carry):
            local = pl.multiple_of(w * DISP, DISP)
            base = pl.multiple_of((part * half1 + w) * DISP, DISP)
            for q in range(FIRST_OUT // LANE):
                value = acc[pl.ds(local, DISP), q * LANE : (q + 1) * LANE]
                value = jnp.maximum(value, 0.0).astype(jnp.bfloat16)
                first_pad[q, 8 : 8 + DISP, :] = value.astype(jnp.float32)
                for e in range(3):
                    lanes = (q // 2) * 3 * PART + e * PART + (q % 2) * LANE
                    if e == 1:
                        moved = value
                    else:
                        moved = first_pad[q, 6 + 2 * e : 6 + 2 * e + DISP, :].astype(jnp.bfloat16)
                    first[pl.ds(base, DISP), lanes : lanes + LANE] = moved
            return carry

        lax.fori_loop(0, half1, column, 0, unroll=True)

    chunks = 3 if (cols + 2) % 3 == 0 else 2
    chunk = (cols + 2) // chunks
    for part in range(chunks):
        for p in range(2):
            lanes = p * 3 * PART
            total = None
            for kw in range(3):
                start = (part * chunk + 2 * kw) * DISP
                term = jnp.dot(
                    first[start : start + chunk * DISP, lanes : lanes + 3 * PART],
                    t2_ref[kw],
                    preferred_element_type=jnp.float32,
                )
                total = term if total is None else total + term
            start = (part * chunk + 2) * DISP
            kept = first[start : start + chunk * DISP, lanes + PART : lanes + 2 * PART]
            total = jnp.maximum(total + kept.astype(jnp.float32), 0.0).astype(jnp.bfloat16)
            start = part * chunk * DISP
            second[start : start + chunk * DISP, p * PART : (p + 1) * PART] = total

    total = None
    for kw in range(3):
        term = jnp.dot(
            second[kw * DISP : (kw + cols) * DISP, :], t3_ref[kw], preferred_element_type=jnp.float32
        )
        total = term if total is None else total + term
    score_pad[8 : 8 + cols * DISP, :] = total
    row = lax.broadcasted_iota(jnp.int32, (DISP, LANE), 0)
    level = ((DISP - 1) - row).astype(jnp.float32)

    def score_column(w, carry):
        base = pl.multiple_of(8 + w * DISP, 8)
        score = jnp.where(row == 0, 0.0, score_pad[pl.ds(base - 1, DISP), :])
        score = score + pltpu.roll(score_pad[pl.ds(base, DISP), :], LANE - ROWS, 1)
        later = jnp.where(row == DISP - 1, 0.0, score_pad[pl.ds(base + 1, DISP), :])
        score = score + pltpu.roll(later, LANE - 2 * ROWS, 1)
        weights = jnp.exp(CAP * jnp.tanh(score / CAP))
        bottom = jnp.sum(weights, axis=0, keepdims=True)
        top = jnp.sum(weights * level, axis=0, keepdims=True)
        out_pad[pl.ds(w, 1), :] = top / bottom / DISP
        return carry

    out_pad[...] = jnp.zeros_like(out_pad)
    score_pad[:8, :] = jnp.zeros((8, LANE), jnp.float32)
    score_pad[8 + cols * DISP :, :] = jnp.zeros((8, LANE), jnp.float32)
    lax.fori_loop(0, cols, score_column, 0, unroll=8)
    out_pad[...] = jnp.transpose(out_pad[...])
    me = lax.axis_index("grp")
    share = ROWS // slots
    for t in range(slots):
        outs[t][...] = out_pad[pl.ds((me ^ t) * share, share), :cols]


def scratch(cols):
    cost_cols = cols + 2 * HALO
    tiles = PER * (WHOLE // LANE + 1)
    return [
        pltpu.VMEM((tiles, cost_cols, LANE), jnp.float32),
        pltpu.VMEM((tiles, cost_cols + SPREAD, LANE), jnp.float32),
        pltpu.VMEM((cost_cols * DISP, DEPTH), jnp.bfloat16),
        pltpu.VMEM((WHOLE // LANE + 1, DISP + 16, LANE), jnp.float32),
    ]


def first_part(feats, t1, slots, cols):
    whole = pl.BlockSpec(memory_space=pltpu.VMEM)
    return pl.pallas_call(
        functools.partial(first_kernel, slots=slots, cols=cols),
        out_shape=jax.ShapeDtypeStruct((2, (cols + 6) // 2 * DISP, FIRST_OUT), jnp.float32),
        in_specs=[whole] * (len(feats) + 1),
        out_specs=whole,
        scratch_shapes=scratch(cols),
        compiler_params=pltpu.CompilerParams(vmem_limit_bytes=16 << 20),
        cost_estimate=pl.CostEstimate(
            flops=7_000_000_000, bytes_accessed=6_000_000, transcendentals=0
        ),
        name="first_part",
    )(*feats, t1)


def aggregate(feats, t1, t2, t3, acc, slots, cols):
    whole = pl.BlockSpec(memory_space=pltpu.VMEM)
    return pl.pallas_call(
        functools.partial(main_kernel, slots=slots, cols=cols),
        out_shape=[jax.ShapeDtypeStruct((ROWS // slots, cols), jnp.float32)] * slots,
        in_specs=[whole] * (len(feats) + 4),
        out_specs=[whole] * slots,
        scratch_shapes=scratch(cols)
        + [
            pltpu.VMEM(((cols + 6) // 2 * DISP, FIRST_OUT), jnp.float32),
            pltpu.VMEM(((cols + 6) * DISP, 3 * FIRST_OUT), jnp.bfloat16),
            pltpu.VMEM((FIRST_OUT // LANE, DISP + 16, LANE), jnp.float32),
            pltpu.VMEM(((cols + 2) * DISP, FIRST_OUT), jnp.bfloat16),
            pltpu.VMEM((cols * DISP + 16, LANE), jnp.float32),
            pltpu.VMEM((LANE, LANE), jnp.float32),
        ],
        compiler_params=pltpu.CompilerParams(vmem_limit_bytes=20 << 20),
        name="aggregate",
    )(*feats, t1, t2, t3, acc)


def assemble_kernel(*refs, slots):
    me = lax.axis_index("grp")
    pieces = [ref[...] for ref in refs[:slots]]
    bit = 1
    while bit < slots:
        swap = (me & bit) > 0
        pieces = [jnp.where(swap, pieces[t ^ bit], pieces[t]) for t in range(slots)]
        bit *= 2
    cols = pieces[0].shape[1]
    for t in range(slots):
        refs[slots][:, t * cols : (t + 1) * cols] = pieces[t]


def assemble(pieces):
    slots = len(pieces)
    rows, cols = pieces[0].shape
    whole = pl.BlockSpec(memory_space=pltpu.VMEM)
    return pl.pallas_call(
        functools.partial(assemble_kernel, slots=slots),
        out_shape=jax.ShapeDtypeStruct((rows, cols * slots), jnp.float32),
        in_specs=[whole] * slots,
        out_specs=whole,
        compiler_params=pltpu.CompilerParams(vmem_limit_bytes=4 << 20),
        name="assemble",
    )(*pieces)


def by_column(block):
    channels, row_count, col_count = block.shape
    grouped = block.reshape(channels // PER, PER, row_count, col_count)
    return jnp.transpose(grouped, (3, 1, 0, 2)).reshape(col_count, channels * row_count)


def passed(value, axis, by):
    peers = lax.axis_size(axis)
    return lax.ppermute(value, axis, [(i, (i + by) % peers) for i in range(peers)])


def per_device(left_feats, right_feats, w_first, w_second, w_out):
    _, row_count, col_count = left_feats.shape
    slots = lax.axis_size("grp")
    me = lax.axis_index("grp")
    cols = col_count // slots
    behind = HALO + SPREAD
    right, left_feats = lax.optimization_barrier((by_column(right_feats), left_feats))
    right_before = passed(right[col_count - behind :], "lon", 1)
    left = lax.optimization_barrier(by_column(left_feats))
    left_before = passed(left[col_count - HALO :], "lon", 1)
    after = passed(jnp.concatenate([right[:HALO], left[:HALO]], axis=0), "lon", -1)

    def partner(value, t):
        return lax.ppermute(value, "grp", [(i, i ^ t) for i in range(slots)]) if t > 0 else value

    def inner(target):
        return jnp.concatenate(
            [lax.dynamic_slice_in_dim(x, target * cols, cols, 0) for x in (right, left)], axis=0
        )

    inners = [partner(inner(me ^ t), t) for t in range(slots)]
    t1a, t1b, t2, t3 = banded_weights(w_first, w_second, w_out, slots)
    left_wide = jnp.concatenate([left_before, left, after[HALO:]], axis=0)
    right_wide = jnp.concatenate([right_before, right, after[:HALO]], axis=0)

    def outer(target):
        start = target * cols
        return jnp.concatenate(
            [
                lax.dynamic_slice_in_dim(right_wide, start, behind, 0),
                lax.dynamic_slice_in_dim(right_wide, start + behind + cols, HALO, 0),
                lax.dynamic_slice_in_dim(left_wide, start, HALO, 0),
                lax.dynamic_slice_in_dim(left_wide, start + HALO + cols, HALO, 0),
            ],
            axis=0,
        )

    outers = [partner(outer(me ^ t), t) for t in range(slots)]
    feats = [x for pair in zip(inners, outers) for x in pair]
    near = 2 * slots // PARTS
    acc = first_part(feats[:near], t1a, slots, cols)
    pieces = aggregate(feats[near:], t1b, t2, t3, acc, slots, cols)
    return assemble([partner(pieces[t], t) for t in range(slots)])


def solution(mesh):
    placed = (P("grp", "pairs", "lon"), P("grp", "pairs", "lon"), P(), P(), P())
    return jax.shard_map(
        per_device,
        mesh=mesh,
        in_specs=placed,
        out_specs=P(("pairs", "grp"), "lon"),
        check_vma=False,
    )
```

```python
import functools

import jax
import jax.numpy as jnp
from jax import lax
from jax.experimental import pallas as pl
from jax.experimental.pallas import tpu as pltpu
from jax.sharding import PartitionSpec as P

C = 320
G = 40
CH = 32
DISP = 48
PER = C // G
ROWS = 16
HALF = ROWS // 2
LANE = 128
HALO = 4
SPREAD = DISP - 1
PARTS = 2
SHARE = G * ROWS // PARTS
WHOLE = SHARE // LANE * LANE
REST = SHARE - WHOLE
DEPTH = 3 * WHOLE + 4 * REST
FIRST_OUT = ROWS * CH
PART = FIRST_OUT // 2
CAP = 12.0
CHUNKS = 6


def weights_kernel(
    w1_ref, w2_ref, w3_ref, t1a_ref, t1b_ref, t2_ref, t3_ref, v1, v3_ref, *, slots
):
    here = G // slots
    me = lax.axis_index("grp")
    quarters = LANE // CH
    for tap in range(27):
        w1 = w1_ref[tap].astype(jnp.float32)
        v1[tap, :, :] = jnp.transpose(jnp.concatenate([w1] * quarters, axis=0))
    row16 = lax.broadcasted_iota(jnp.int32, (ROWS, LANE), 0)
    quarter = lax.broadcasted_iota(jnp.int32, (ROWS, LANE), 1) // CH
    masks = []
    for q in range(FIRST_OUT // LANE):
        at = quarters * q + quarter
        out_row = 2 * (at % HALF) + at // HALF
        masks.append(
            [jnp.where(row16 == out_row + kh - 1, 1.0, 0.0).astype(jnp.bfloat16) for kh in range(3)]
        )
    per_part = slots // PARTS
    for part, t1_ref in enumerate((t1a_ref, t1b_ref)):
        for kw in range(3):

            def one_tap(t, carry):
                e, slot = t // per_part, t % per_part
                tap = (2 - e) * 9 + kw
                group = (me ^ (part * per_part + slot)) * here
                for i in range(here):
                    rows = []
                    for kh in range(3):
                        row = v1[tap + 3 * kh, pl.ds(group + i, 1), :]
                        rows.append(jnp.broadcast_to(row, (ROWS, LANE)).astype(jnp.bfloat16))
                    at = (slot * here + i) * ROWS
                    start = jnp.where(at < WHOLE, e * WHOLE + at, 3 * WHOLE + e * REST + at - WHOLE)
                    start = pl.multiple_of(start, ROWS)
                    for q in range(FIRST_OUT // LANE):
                        value = (
                            masks[q][0] * rows[0] + masks[q][1] * rows[1] + masks[q][2] * rows[2]
                        )
                        t1_ref[kw, pl.ds(start, ROWS), q * LANE : (q + 1) * LANE] = value
                return carry

            lax.fori_loop(0, 3 * per_part, one_tap, 0)
            t1_ref[kw, DEPTH - REST :, :] = jnp.zeros((REST, FIRST_OUT), jnp.bfloat16)

    lane32 = lax.broadcasted_iota(jnp.int32, (CH, LANE), 1) // CH
    for kw in range(3):
        for e in range(3):
            tap = (2 - e) * 9 + kw
            v2 = [
                jnp.transpose(
                    jnp.concatenate([w2_ref[tap + 3 * kh].astype(jnp.float32)] * quarters, axis=0)
                )
                for kh in range(3)
            ]
            for hi in range(HALF):
                for q in range(PART // LANE):
                    value = jnp.zeros((CH, LANE), jnp.float32)
                    for kh in range(3):
                        if quarters * q <= hi - kh + 1 < quarters * (q + 1):
                            value = jnp.where(quarters * q + lane32 == hi - kh + 1, v2[kh], value)
                    start = e * PART + hi * CH
                    t2_ref[kw, start : start + CH, q * LANE : (q + 1) * LANE] = value.astype(
                        jnp.bfloat16
                    )

    v3_ref[...] = jnp.zeros_like(v3_ref)
    for i in range(9):
        v3_ref[3 * i : 3 * i + 3, :CH] = w3_ref[i].astype(jnp.float32)
    taps = jnp.transpose(v3_ref[...])[:CH]
    out_lane = lax.broadcasted_iota(jnp.int32, (CH, LANE), 1)
    for kw in range(3):
        v3 = []
        for kh in range(3):
            value = jnp.zeros((CH, LANE), jnp.float32)
            for e in range(3):
                tap = (2 - e) * 9 + 3 * kh + kw
                column = jnp.broadcast_to(taps[:, tap : tap + 1], (CH, LANE))
                value = jnp.where(out_lane // ROWS == e, column, value)
            v3.append(value)
        for at in range(ROWS):
            hi = 2 * (at % HALF) + at // HALF
            value = jnp.zeros((CH, LANE), jnp.float32)
            for kh in range(3):
                value = jnp.where(out_lane % ROWS == hi - kh + 1, v3[kh], value)
            t3_ref[kw, at * CH : (at + 1) * CH, :] = value.astype(jnp.bfloat16)


def banded_weights(w_first, w_second, w_out, slots):
    w1 = jnp.transpose(w_first, (2, 3, 4, 0, 1)).reshape(27, CH, G)
    w2 = jnp.transpose(w_second, (2, 3, 4, 0, 1)).reshape(27, CH, CH)
    w3 = jnp.transpose(w_out, (0, 2, 3, 4, 1)).reshape(9, 3, CH)
    whole = pl.BlockSpec(memory_space=pltpu.VMEM)
    shapes = [
        (3, DEPTH, FIRST_OUT),
        (3, DEPTH, FIRST_OUT),
        (3, 3 * PART, PART),
        (3, FIRST_OUT, LANE),
    ]
    return pl.pallas_call(
        functools.partial(weights_kernel, slots=slots),
        out_shape=tuple(jax.ShapeDtypeStruct(shape, jnp.bfloat16) for shape in shapes),
        in_specs=[whole, whole, whole],
        out_specs=[whole] * 4,
        scratch_shapes=[
            pltpu.VMEM((27, G, LANE), jnp.float32),
            pltpu.VMEM((LANE, LANE), jnp.float32),
        ],
        compiler_params=pltpu.CompilerParams(vmem_limit_bytes=8 << 20),
        cost_estimate=pl.CostEstimate(flops=9_000_000, bytes_accessed=8_000_000, transcendentals=0),
        name="banded_weights",
    )(w1, w2, w3)


def unpack(feats, left, right, slots, cols):
    span = G // slots * ROWS
    blocks = WHOLE // LANE
    behind = HALO + SPREAD

    def joined(refs, k):
        pieces = [ref[:, k * span : (k + 1) * span].astype(jnp.float32) for ref in refs]
        pieces.append(jnp.zeros((pieces[0].shape[0], LANE - REST), jnp.float32))
        return jnp.concatenate(pieces, axis=1)

    for k in range(PER):
        inner, outer = joined(feats[0::2], k), joined(feats[1::2], k)
        for j in range(blocks + 1):
            at = k * (blocks + 1) + j
            mine = inner[:, j * LANE : (j + 1) * LANE]
            edge = outer[:, j * LANE : (j + 1) * LANE]
            right[at, :behind, :] = edge[:behind]
            right[at, behind : behind + cols, :] = mine[:cols]
            right[at, behind + cols :, :] = edge[behind : behind + HALO]
            left[at, :HALO, :] = edge[behind + HALO : behind + 2 * HALO]
            left[at, HALO : HALO + cols, :] = mine[cols:]
            left[at, HALO + cols :, :] = edge[behind + 2 * HALO :]


def cost_columns(first_column, last_column, left, right, cells, cost_pad):
    blocks = WHOLE // LANE
    for w in range(first_column, last_column):
        rows = slice(w * DISP, (w + 1) * DISP)
        for j in range(blocks + 1):
            total = None
            for k in range(PER):
                at = k * (blocks + 1) + j
                l_row = jnp.broadcast_to(left[at, w : w + 1, :], (DISP, LANE))
                term = l_row * right[at, w : w + DISP, :]
                total = term if total is None else total + term
            total = (total * (1.0 / PER)).astype(jnp.bfloat16)
            wide = total.astype(jnp.float32)
            pad = cost_pad.at[w % 2, j]
            pad[8 : 8 + DISP, :] = wide
            moved = [pad[7 : 7 + DISP, :], wide, pad[9 : 9 + DISP, :]]
            if j < blocks:
                for e in range(3):
                    lanes = e * WHOLE + j * LANE
                    cells[rows, lanes : lanes + LANE] = moved[e].astype(jnp.bfloat16)
            else:
                pair = moved[0] + pltpu.roll(moved[1], REST, 1)
                lanes = 3 * WHOLE
                cells[rows, lanes : lanes + LANE] = pair.astype(jnp.bfloat16)
                lanes += LANE
                cells[rows, lanes : lanes + LANE] = moved[2].astype(jnp.bfloat16)


def bounds_of(count, chunks):
    return [count * i // chunks for i in range(chunks + 1)]


def first_kernel(*refs, slots, cols):
    count = 2 * slots // PARTS
    t1_ref, acc, left, right, cells, cost_pad = refs[count:]
    unpack(refs[:count], left, right, slots, cols)
    cost_pad[...] = jnp.zeros_like(cost_pad)
    bounds = bounds_of(cols + 6, CHUNKS)
    cost_columns(0, bounds[1] + 2, left, right, cells, cost_pad)
    for i in range(CHUNKS):
        if i + 1 < CHUNKS:
            cost_columns(bounds[i + 1] + 2, bounds[i + 2] + 2, left, right, cells, cost_pad)
        low, high = bounds[i], bounds[i + 1]
        total = None
        for kw in range(3):
            term = jnp.dot(
                cells[(low + kw) * DISP : (high + kw) * DISP, :],
                t1_ref[kw],
                preferred_element_type=jnp.float32,
            )
            total = term if total is None else total + term
        acc[low * DISP : high * DISP, :] = total


def main_kernel(*refs, slots, cols):
    count = 2 * slots // PARTS
    t1_ref, t2_ref, t3_ref, acc_ref = refs[count : count + 4]
    outs = refs[count + 4 : count + 4 + slots]
    (
        left, right, cells, cost_pad, acc, first, first_pad, second, score_pad, out_pad,
    ) = refs[count + 4 + slots :]
    unpack(refs[:count], left, right, slots, cols)
    cost_pad[...] = jnp.zeros_like(cost_pad)
    first_pad[...] = jnp.zeros_like(first_pad)
    bounds = bounds_of(cols + 6, CHUNKS)
    cost_columns(0, bounds[1] + 2, left, right, cells, cost_pad)
    for i in range(CHUNKS):
        if i + 1 < CHUNKS:
            cost_columns(bounds[i + 1] + 2, bounds[i + 2] + 2, left, right, cells, cost_pad)
        low, high = bounds[i], bounds[i + 1]
        total = acc_ref[low * DISP : high * DISP, :]
        for kw in range(3):
            total = total + jnp.dot(
                cells[(low + kw) * DISP : (high + kw) * DISP, :],
                t1_ref[kw],
                preferred_element_type=jnp.float32,
            )
        acc[low * DISP : high * DISP, :] = total
        for w in range(low, high):
            rows = slice(w * DISP, (w + 1) * DISP)
            for q in range(FIRST_OUT // LANE):
                value = acc[rows, q * LANE : (q + 1) * LANE]
                value = jnp.maximum(value, 0.0).astype(jnp.bfloat16)
                pad = first_pad.at[w % 2, q]
                pad[8 : 8 + DISP, :] = value.astype(jnp.float32)
                for e in range(3):
                    lanes = (q // 2) * 3 * PART + e * PART + (q % 2) * LANE
                    if e == 1:
                        moved = value
                    else:
                        moved = pad[6 + 2 * e : 6 + 2 * e + DISP, :].astype(jnp.bfloat16)
                    first[rows, lanes : lanes + LANE] = moved

    chunks = 3 if (cols + 2) % 3 == 0 else 2
    chunk = (cols + 2) // chunks
    for part in range(chunks):
        for p in range(2):
            lanes = p * 3 * PART
            total = None
            for kw in range(3):
                start = (part * chunk + 2 * kw) * DISP
                term = jnp.dot(
                    first[start : start + chunk * DISP, lanes : lanes + 3 * PART],
                    t2_ref[kw],
                    preferred_element_type=jnp.float32,
                )
                total = term if total is None else total + term
            start = (part * chunk + 2) * DISP
            kept = first[start : start + chunk * DISP, lanes + PART : lanes + 2 * PART]
            total = jnp.maximum(total + kept.astype(jnp.float32), 0.0).astype(jnp.bfloat16)
            start = part * chunk * DISP
            second[start : start + chunk * DISP, p * PART : (p + 1) * PART] = total

    total = None
    for kw in range(3):
        term = jnp.dot(
            second[kw * DISP : (kw + cols) * DISP, :], t3_ref[kw], preferred_element_type=jnp.float32
        )
        total = term if total is None else total + term
    score_pad[8 : 8 + cols * DISP, :] = total
    row = lax.broadcasted_iota(jnp.int32, (DISP, LANE), 0)
    level = ((DISP - 1) - row).astype(jnp.float32)

    def score_column(w, carry):
        base = pl.multiple_of(8 + w * DISP, 8)
        score = jnp.where(row == 0, 0.0, score_pad[pl.ds(base - 1, DISP), :])
        score = score + pltpu.roll(score_pad[pl.ds(base, DISP), :], LANE - ROWS, 1)
        later = jnp.where(row == DISP - 1, 0.0, score_pad[pl.ds(base + 1, DISP), :])
        score = score + pltpu.roll(later, LANE - 2 * ROWS, 1)
        weights = jnp.exp(CAP * jnp.tanh(score / CAP))
        bottom = jnp.sum(weights, axis=0, keepdims=True)
        top = jnp.sum(weights * level, axis=0, keepdims=True)
        out_pad[pl.ds(w, 1), :] = top / bottom / DISP
        return carry

    out_pad[...] = jnp.zeros_like(out_pad)
    score_pad[:8, :] = jnp.zeros((8, LANE), jnp.float32)
    score_pad[8 + cols * DISP :, :] = jnp.zeros((8, LANE), jnp.float32)
    lax.fori_loop(0, cols, score_column, 0, unroll=8)
    out_pad[...] = jnp.transpose(out_pad[...])
    me = lax.axis_index("grp")
    share = ROWS // slots
    for t in range(slots):
        outs[t][...] = out_pad[pl.ds((me ^ t) * share, share), :cols]


def scratch(cols):
    cost_cols = cols + 2 * HALO
    tiles = PER * (WHOLE // LANE + 1)
    return [
        pltpu.VMEM((tiles, cost_cols, LANE), jnp.float32),
        pltpu.VMEM((tiles, cost_cols + SPREAD, LANE), jnp.float32),
        pltpu.VMEM((cost_cols * DISP, DEPTH), jnp.bfloat16),
        pltpu.VMEM((2, WHOLE // LANE + 1, DISP + 16, LANE), jnp.float32),
    ]


def first_part(feats, t1, slots, cols):
    whole = pl.BlockSpec(memory_space=pltpu.VMEM)
    return pl.pallas_call(
        functools.partial(first_kernel, slots=slots, cols=cols),
        out_shape=jax.ShapeDtypeStruct(((cols + 6) * DISP, FIRST_OUT), jnp.float32),
        in_specs=[whole] * (len(feats) + 1),
        out_specs=whole,
        scratch_shapes=scratch(cols),
        compiler_params=pltpu.CompilerParams(vmem_limit_bytes=16 << 20),
        cost_estimate=pl.CostEstimate(
            flops=7_000_000_000, bytes_accessed=6_000_000, transcendentals=0
        ),
        name="first_part",
    )(*feats, t1)


def aggregate(feats, t1, t2, t3, acc, slots, cols):
    whole = pl.BlockSpec(memory_space=pltpu.VMEM)
    return pl.pallas_call(
        functools.partial(main_kernel, slots=slots, cols=cols),
        out_shape=[jax.ShapeDtypeStruct((ROWS // slots, cols), jnp.float32)] * slots,
        in_specs=[whole] * (len(feats) + 4),
        out_specs=[whole] * slots,
        scratch_shapes=scratch(cols)
        + [
            pltpu.VMEM(((cols + 6) * DISP, FIRST_OUT), jnp.float32),
            pltpu.VMEM(((cols + 6) * DISP, 3 * FIRST_OUT), jnp.bfloat16),
            pltpu.VMEM((2, FIRST_OUT // LANE, DISP + 16, LANE), jnp.float32),
            pltpu.VMEM(((cols + 2) * DISP, FIRST_OUT), jnp.bfloat16),
            pltpu.VMEM((cols * DISP + 16, LANE), jnp.float32),
            pltpu.VMEM((LANE, LANE), jnp.float32),
        ],
        compiler_params=pltpu.CompilerParams(vmem_limit_bytes=20 << 20),
        name="aggregate",
    )(*feats, t1, t2, t3, acc)


def assemble_kernel(*refs, slots):
    me = lax.axis_index("grp")
    pieces = [ref[...] for ref in refs[:slots]]
    bit = 1
    while bit < slots:
        swap = (me & bit) > 0
        pieces = [jnp.where(swap, pieces[t ^ bit], pieces[t]) for t in range(slots)]
        bit *= 2
    cols = pieces[0].shape[1]
    for t in range(slots):
        refs[slots][:, t * cols : (t + 1) * cols] = pieces[t]


def assemble(pieces):
    slots = len(pieces)
    rows, cols = pieces[0].shape
    whole = pl.BlockSpec(memory_space=pltpu.VMEM)
    return pl.pallas_call(
        functools.partial(assemble_kernel, slots=slots),
        out_shape=jax.ShapeDtypeStruct((rows, cols * slots), jnp.float32),
        in_specs=[whole] * slots,
        out_specs=whole,
        compiler_params=pltpu.CompilerParams(vmem_limit_bytes=4 << 20),
        name="assemble",
    )(*pieces)


def by_column(block):
    channels, row_count, col_count = block.shape
    grouped = block.reshape(channels // PER, PER, row_count, col_count)
    return jnp.transpose(grouped, (3, 1, 0, 2)).reshape(col_count, channels * row_count)


def passed(value, axis, by):
    peers = lax.axis_size(axis)
    return lax.ppermute(value, axis, [(i, (i + by) % peers) for i in range(peers)])


def per_device(left_feats, right_feats, w_first, w_second, w_out):
    _, row_count, col_count = left_feats.shape
    slots = lax.axis_size("grp")
    me = lax.axis_index("grp")
    cols = col_count // slots
    behind = HALO + SPREAD
    right, left_feats = lax.optimization_barrier((by_column(right_feats), left_feats))
    left = lax.optimization_barrier(by_column(left_feats))
    before = passed(
        jnp.concatenate([right[col_count - behind :], left[col_count - HALO :]], axis=0), "lon", 1
    )
    right_before, left_before = before[:behind], before[behind:]
    after = passed(jnp.concatenate([right[:HALO], left[:HALO]], axis=0), "lon", -1)

    def partner(value, t):
        return lax.ppermute(value, "grp", [(i, i ^ t) for i in range(slots)]) if t > 0 else value

    def inner(target):
        return jnp.concatenate(
            [lax.dynamic_slice_in_dim(x, target * cols, cols, 0) for x in (right, left)], axis=0
        )

    inners = [partner(inner(me ^ t), t) for t in range(slots)]
    t1a, t1b, t2, t3 = banded_weights(w_first, w_second, w_out, slots)
    left_wide = jnp.concatenate([left_before, left, after[HALO:]], axis=0)
    right_wide = jnp.concatenate([right_before, right, after[:HALO]], axis=0)

    def outer(target):
        start = target * cols
        return jnp.concatenate(
            [
                lax.dynamic_slice_in_dim(right_wide, start, behind, 0),
                lax.dynamic_slice_in_dim(right_wide, start + behind + cols, HALO, 0),
                lax.dynamic_slice_in_dim(left_wide, start, HALO, 0),
                lax.dynamic_slice_in_dim(left_wide, start + HALO + cols, HALO, 0),
            ],
            axis=0,
        )

    outers = [partner(outer(me ^ t), t) for t in range(slots)]
    feats = [x for pair in zip(inners, outers) for x in pair]
    near = 2 * slots // PARTS
    acc = first_part(feats[:near], t1a, slots, cols)
    pieces = aggregate(feats[near:], t1b, t2, t3, acc, slots, cols)
    return assemble([partner(pieces[t], t) for t in range(slots)])


def solution(mesh):
    placed = (P("grp", "pairs", "lon"), P("grp", "pairs", "lon"), P(), P(), P())
    return jax.shard_map(
        per_device,
        mesh=mesh,
        in_specs=placed,
        out_specs=P(("pairs", "grp"), "lon"),
        check_vma=False,
    )
```

```python
import functools

import jax
import jax.numpy as jnp
from jax import lax
from jax.experimental import pallas as pl
from jax.experimental.pallas import tpu as pltpu
from jax.sharding import PartitionSpec as P

C = 320
G = 40
CH = 32
DISP = 48
PER = C // G
ROWS = 16
HALF = ROWS // 2
LANE = 128
HALO = 4
SPREAD = DISP - 1
PARTS = 2
SHARE = G * ROWS // PARTS
WHOLE = SHARE // LANE * LANE
REST = SHARE - WHOLE
DEPTH = 3 * WHOLE + 4 * REST
FIRST_OUT = ROWS * CH
PART = FIRST_OUT // 2
CAP = 12.0
CHUNKS = 6


def weights_kernel(
    w1_ref, w2_ref, w3_ref, t1a_ref, t1b_ref, t2_ref, t3_ref, v1, v3_ref, *, slots
):
    here = G // slots
    me = lax.axis_index("grp")
    quarters = LANE // CH
    for tap in range(27):
        w1 = w1_ref[tap].astype(jnp.float32)
        v1[tap, :, :] = jnp.transpose(jnp.concatenate([w1] * quarters, axis=0))
    row16 = lax.broadcasted_iota(jnp.int32, (ROWS, LANE), 0)
    quarter = lax.broadcasted_iota(jnp.int32, (ROWS, LANE), 1) // CH
    masks = []
    for q in range(FIRST_OUT // LANE):
        at = quarters * q + quarter
        out_row = 2 * (at % HALF) + at // HALF
        masks.append(
            [jnp.where(row16 == out_row + kh - 1, 1.0, 0.0).astype(jnp.bfloat16) for kh in range(3)]
        )
    per_part = slots // PARTS
    for part, t1_ref in enumerate((t1a_ref, t1b_ref)):
        for kw in range(3):

            def one_tap(t, carry):
                e, slot = t // per_part, t % per_part
                tap = (2 - e) * 9 + kw
                group = (me ^ (part * per_part + slot)) * here
                for i in range(here):
                    rows = []
                    for kh in range(3):
                        row = v1[tap + 3 * kh, pl.ds(group + i, 1), :]
                        rows.append(jnp.broadcast_to(row, (ROWS, LANE)).astype(jnp.bfloat16))
                    at = (slot * here + i) * ROWS
                    start = jnp.where(at < WHOLE, e * WHOLE + at, 3 * WHOLE + e * REST + at - WHOLE)
                    start = pl.multiple_of(start, ROWS)
                    for q in range(FIRST_OUT // LANE):
                        value = (
                            masks[q][0] * rows[0] + masks[q][1] * rows[1] + masks[q][2] * rows[2]
                        )
                        t1_ref[kw, pl.ds(start, ROWS), q * LANE : (q + 1) * LANE] = value
                return carry

            lax.fori_loop(0, 3 * per_part, one_tap, 0)
            t1_ref[kw, DEPTH - REST :, :] = jnp.zeros((REST, FIRST_OUT), jnp.bfloat16)

    lane32 = lax.broadcasted_iota(jnp.int32, (CH, LANE), 1) // CH
    for kw in range(3):
        for e in range(3):
            tap = (2 - e) * 9 + kw
            v2 = [
                jnp.transpose(
                    jnp.concatenate([w2_ref[tap + 3 * kh].astype(jnp.float32)] * quarters, axis=0)
                )
                for kh in range(3)
            ]
            for hi in range(HALF):
                for q in range(PART // LANE):
                    value = jnp.zeros((CH, LANE), jnp.float32)
                    for kh in range(3):
                        if quarters * q <= hi - kh + 1 < quarters * (q + 1):
                            value = jnp.where(quarters * q + lane32 == hi - kh + 1, v2[kh], value)
                    start = e * PART + hi * CH
                    t2_ref[kw, start : start + CH, q * LANE : (q + 1) * LANE] = value.astype(
                        jnp.bfloat16
                    )

    v3_ref[...] = jnp.zeros_like(v3_ref)
    for i in range(9):
        v3_ref[3 * i : 3 * i + 3, :CH] = w3_ref[i].astype(jnp.float32)
    taps = jnp.transpose(v3_ref[...])[:CH]
    out_lane = lax.broadcasted_iota(jnp.int32, (CH, LANE), 1)
    for kw in range(3):
        v3 = []
        for kh in range(3):
            value = jnp.zeros((CH, LANE), jnp.float32)
            for e in range(3):
                tap = (2 - e) * 9 + 3 * kh + kw
                column = jnp.broadcast_to(taps[:, tap : tap + 1], (CH, LANE))
                value = jnp.where(out_lane // ROWS == e, column, value)
            v3.append(value)
        for at in range(ROWS):
            hi = 2 * (at % HALF) + at // HALF
            value = jnp.zeros((CH, LANE), jnp.float32)
            for kh in range(3):
                value = jnp.where(out_lane % ROWS == hi - kh + 1, v3[kh], value)
            t3_ref[kw, at * CH : (at + 1) * CH, :] = value.astype(jnp.bfloat16)


def banded_weights(w_first, w_second, w_out, slots):
    w1 = jnp.transpose(w_first, (2, 3, 4, 0, 1)).reshape(27, CH, G)
    w2 = jnp.transpose(w_second, (2, 3, 4, 0, 1)).reshape(27, CH, CH)
    w3 = jnp.transpose(w_out, (0, 2, 3, 4, 1)).reshape(9, 3, CH)
    whole = pl.BlockSpec(memory_space=pltpu.VMEM)
    shapes = [
        (3, DEPTH, FIRST_OUT),
        (3, DEPTH, FIRST_OUT),
        (3, 3 * PART, PART),
        (3, FIRST_OUT, LANE),
    ]
    return pl.pallas_call(
        functools.partial(weights_kernel, slots=slots),
        out_shape=tuple(jax.ShapeDtypeStruct(shape, jnp.bfloat16) for shape in shapes),
        in_specs=[whole, whole, whole],
        out_specs=[whole] * 4,
        scratch_shapes=[
            pltpu.VMEM((27, G, LANE), jnp.float32),
            pltpu.VMEM((LANE, LANE), jnp.float32),
        ],
        compiler_params=pltpu.CompilerParams(vmem_limit_bytes=8 << 20),
        cost_estimate=pl.CostEstimate(flops=9_000_000, bytes_accessed=8_000_000, transcendentals=0),
        name="banded_weights",
    )(w1, w2, w3)


def unpack(feats, left, right, slots, cols):
    span = G // slots * ROWS
    blocks = WHOLE // LANE
    behind = HALO + SPREAD

    def joined(refs, k):
        pieces = [ref[:, k * span : (k + 1) * span].astype(jnp.float32) for ref in refs]
        pieces.append(jnp.zeros((pieces[0].shape[0], LANE - REST), jnp.float32))
        return jnp.concatenate(pieces, axis=1)

    for k in range(PER):
        inner, outer = joined(feats[0::2], k), joined(feats[1::2], k)
        for j in range(blocks + 1):
            at = k * (blocks + 1) + j
            mine = inner[:, j * LANE : (j + 1) * LANE]
            edge = outer[:, j * LANE : (j + 1) * LANE]
            right[at, :behind, :] = edge[:behind]
            right[at, behind : behind + cols, :] = mine[:cols]
            right[at, behind + cols :, :] = edge[behind : behind + HALO]
            left[at, :HALO, :] = edge[behind + HALO : behind + 2 * HALO]
            left[at, HALO : HALO + cols, :] = mine[cols:]
            left[at, HALO + cols :, :] = edge[behind + 2 * HALO :]


def cost_columns(first_column, last_column, left, right, cells, cost_pad):
    blocks = WHOLE // LANE
    for w in range(first_column, last_column):
        rows = slice(w * DISP, (w + 1) * DISP)
        for j in range(blocks + 1):
            total = None
            for k in range(PER):
                at = k * (blocks + 1) + j
                l_row = jnp.broadcast_to(left[at, w : w + 1, :], (DISP, LANE))
                term = l_row * right[at, w : w + DISP, :]
                total = term if total is None else total + term
            total = (total * (1.0 / PER)).astype(jnp.bfloat16)
            wide = total.astype(jnp.float32)
            pad = cost_pad.at[w % 2, j]
            pad[8 : 8 + DISP, :] = wide
            moved = [pad[7 : 7 + DISP, :], wide, pad[9 : 9 + DISP, :]]
            if j < blocks:
                for e in range(3):
                    lanes = e * WHOLE + j * LANE
                    cells[rows, lanes : lanes + LANE] = moved[e].astype(jnp.bfloat16)
            else:
                pair = moved[0] + pltpu.roll(moved[1], REST, 1)
                lanes = 3 * WHOLE
                cells[rows, lanes : lanes + LANE] = pair.astype(jnp.bfloat16)
                lanes += LANE
                cells[rows, lanes : lanes + LANE] = moved[2].astype(jnp.bfloat16)


def bounds_of(count, chunks):
    return [count * i // chunks for i in range(chunks + 1)]


def first_kernel(*refs, slots, cols):
    count = 2 * slots // PARTS
    t1_ref, acc, left, right, cells, cost_pad = refs[count:]
    unpack(refs[:count], left, right, slots, cols)
    cost_pad[...] = jnp.zeros_like(cost_pad)
    bounds = bounds_of(cols + 6, CHUNKS)
    cost_columns(0, bounds[1] + 2, left, right, cells, cost_pad)
    for i in range(CHUNKS):
        if i + 1 < CHUNKS:
            cost_columns(bounds[i + 1] + 2, bounds[i + 2] + 2, left, right, cells, cost_pad)
        low, high = bounds[i], bounds[i + 1]
        total = None
        for kw in range(3):
            term = jnp.dot(
                cells[(low + kw) * DISP : (high + kw) * DISP, :],
                t1_ref[kw],
                preferred_element_type=jnp.float32,
            )
            total = term if total is None else total + term
        acc[low * DISP : high * DISP, :] = total


def main_kernel(*refs, slots, cols):
    count = 2 * slots // PARTS
    t1_ref, t2_ref, t3_ref, acc_ref = refs[count : count + 4]
    outs = refs[count + 4 : count + 4 + slots]
    (
        left, right, cells, cost_pad, acc, first, first_pad, second, score_pad, out_pad,
    ) = refs[count + 4 + slots :]
    unpack(refs[:count], left, right, slots, cols)
    cost_pad[...] = jnp.zeros_like(cost_pad)
    first_pad[...] = jnp.zeros_like(first_pad)
    bounds = bounds_of(cols + 6, CHUNKS)
    cost_columns(0, bounds[1] + 2, left, right, cells, cost_pad)
    for i in range(CHUNKS):
        if i + 1 < CHUNKS:
            cost_columns(bounds[i + 1] + 2, bounds[i + 2] + 2, left, right, cells, cost_pad)
        low, high = bounds[i], bounds[i + 1]
        total = acc_ref[low * DISP : high * DISP, :]
        for kw in range(3):
            total = total + jnp.dot(
                cells[(low + kw) * DISP : (high + kw) * DISP, :],
                t1_ref[kw],
                preferred_element_type=jnp.float32,
            )
        acc[low * DISP : high * DISP, :] = total
        for w in range(low, high):
            rows = slice(w * DISP, (w + 1) * DISP)
            for q in range(FIRST_OUT // LANE):
                value = acc[rows, q * LANE : (q + 1) * LANE]
                value = jnp.maximum(value, 0.0).astype(jnp.bfloat16)
                pad = first_pad.at[w % 2, q]
                pad[8 : 8 + DISP, :] = value.astype(jnp.float32)
                for e in range(3):
                    lanes = (q // 2) * 3 * PART + e * PART + (q % 2) * LANE
                    if e == 1:
                        moved = value
                    else:
                        moved = pad[6 + 2 * e : 6 + 2 * e + DISP, :].astype(jnp.bfloat16)
                    first[rows, lanes : lanes + LANE] = moved

    chunks = 6 if (cols + 2) % 6 == 0 else 2
    chunk = (cols + 2) // chunks
    for part in range(chunks):
        for p in range(2):
            lanes = p * 3 * PART
            total = None
            for kw in range(3):
                start = (part * chunk + 2 * kw) * DISP
                term = jnp.dot(
                    first[start : start + chunk * DISP, lanes : lanes + 3 * PART],
                    t2_ref[kw],
                    preferred_element_type=jnp.float32,
                )
                total = term if total is None else total + term
            start = (part * chunk + 2) * DISP
            kept = first[start : start + chunk * DISP, lanes + PART : lanes + 2 * PART]
            total = jnp.maximum(total + kept.astype(jnp.float32), 0.0).astype(jnp.bfloat16)
            start = part * chunk * DISP
            second[start : start + chunk * DISP, p * PART : (p + 1) * PART] = total

    total = None
    for kw in range(3):
        term = jnp.dot(
            second[kw * DISP : (kw + cols) * DISP, :], t3_ref[kw], preferred_element_type=jnp.float32
        )
        total = term if total is None else total + term
    score_pad[8 : 8 + cols * DISP, :] = total
    row = lax.broadcasted_iota(jnp.int32, (DISP, LANE), 0)
    level = ((DISP - 1) - row).astype(jnp.float32)

    def score_column(w, carry):
        base = pl.multiple_of(8 + w * DISP, 8)
        score = jnp.where(row == 0, 0.0, score_pad[pl.ds(base - 1, DISP), :])
        score = score + pltpu.roll(score_pad[pl.ds(base, DISP), :], LANE - ROWS, 1)
        later = jnp.where(row == DISP - 1, 0.0, score_pad[pl.ds(base + 1, DISP), :])
        score = score + pltpu.roll(later, LANE - 2 * ROWS, 1)
        weights = jnp.exp(CAP * jnp.tanh(score / CAP))
        bottom = jnp.sum(weights, axis=0, keepdims=True)
        top = jnp.sum(weights * level, axis=0, keepdims=True)
        out_pad[pl.ds(w, 1), :] = top / bottom / DISP
        return carry

    out_pad[...] = jnp.zeros_like(out_pad)
    score_pad[:8, :] = jnp.zeros((8, LANE), jnp.float32)
    score_pad[8 + cols * DISP :, :] = jnp.zeros((8, LANE), jnp.float32)
    lax.fori_loop(0, cols, score_column, 0, unroll=True)
    out_pad[...] = jnp.transpose(out_pad[...])
    me = lax.axis_index("grp")
    share = ROWS // slots
    for t in range(slots):
        outs[t][...] = out_pad[pl.ds((me ^ t) * share, share), :cols]


def scratch(cols):
    cost_cols = cols + 2 * HALO
    tiles = PER * (WHOLE // LANE + 1)
    return [
        pltpu.VMEM((tiles, cost_cols, LANE), jnp.float32),
        pltpu.VMEM((tiles, cost_cols + SPREAD, LANE), jnp.float32),
        pltpu.VMEM((cost_cols * DISP, DEPTH), jnp.bfloat16),
        pltpu.VMEM((2, WHOLE // LANE + 1, DISP + 16, LANE), jnp.float32),
    ]


def first_part(feats, t1, slots, cols):
    whole = pl.BlockSpec(memory_space=pltpu.VMEM)
    return pl.pallas_call(
        functools.partial(first_kernel, slots=slots, cols=cols),
        out_shape=jax.ShapeDtypeStruct(((cols + 6) * DISP, FIRST_OUT), jnp.float32),
        in_specs=[whole] * (len(feats) + 1),
        out_specs=whole,
        scratch_shapes=scratch(cols),
        compiler_params=pltpu.CompilerParams(vmem_limit_bytes=16 << 20),
        cost_estimate=pl.CostEstimate(
            flops=7_000_000_000, bytes_accessed=6_000_000, transcendentals=0
        ),
        name="first_part",
    )(*feats, t1)


def aggregate(feats, t1, t2, t3, acc, slots, cols):
    whole = pl.BlockSpec(memory_space=pltpu.VMEM)
    return pl.pallas_call(
        functools.partial(main_kernel, slots=slots, cols=cols),
        out_shape=[jax.ShapeDtypeStruct((ROWS // slots, cols), jnp.float32)] * slots,
        in_specs=[whole] * (len(feats) + 4),
        out_specs=[whole] * slots,
        scratch_shapes=scratch(cols)
        + [
            pltpu.VMEM(((cols + 6) * DISP, FIRST_OUT), jnp.float32),
            pltpu.VMEM(((cols + 6) * DISP, 3 * FIRST_OUT), jnp.bfloat16),
            pltpu.VMEM((2, FIRST_OUT // LANE, DISP + 16, LANE), jnp.float32),
            pltpu.VMEM(((cols + 2) * DISP, FIRST_OUT), jnp.bfloat16),
            pltpu.VMEM((cols * DISP + 16, LANE), jnp.float32),
            pltpu.VMEM((LANE, LANE), jnp.float32),
        ],
        compiler_params=pltpu.CompilerParams(vmem_limit_bytes=20 << 20),
        name="aggregate",
    )(*feats, t1, t2, t3, acc)


def assemble_kernel(*refs, slots):
    me = lax.axis_index("grp")
    pieces = [ref[...] for ref in refs[:slots]]
    bit = 1
    while bit < slots:
        swap = (me & bit) > 0
        pieces = [jnp.where(swap, pieces[t ^ bit], pieces[t]) for t in range(slots)]
        bit *= 2
    cols = pieces[0].shape[1]
    for t in range(slots):
        refs[slots][:, t * cols : (t + 1) * cols] = pieces[t]


def assemble(pieces):
    slots = len(pieces)
    rows, cols = pieces[0].shape
    whole = pl.BlockSpec(memory_space=pltpu.VMEM)
    return pl.pallas_call(
        functools.partial(assemble_kernel, slots=slots),
        out_shape=jax.ShapeDtypeStruct((rows, cols * slots), jnp.float32),
        in_specs=[whole] * slots,
        out_specs=whole,
        compiler_params=pltpu.CompilerParams(vmem_limit_bytes=4 << 20),
        name="assemble",
    )(*pieces)


def by_column(block):
    channels, row_count, col_count = block.shape
    grouped = block.reshape(channels // PER, PER, row_count, col_count)
    return jnp.transpose(grouped, (3, 1, 0, 2)).reshape(col_count, channels * row_count)


def passed(value, axis, by):
    peers = lax.axis_size(axis)
    return lax.ppermute(value, axis, [(i, (i + by) % peers) for i in range(peers)])


def per_device(left_feats, right_feats, w_first, w_second, w_out):
    _, row_count, col_count = left_feats.shape
    slots = lax.axis_size("grp")
    me = lax.axis_index("grp")
    cols = col_count // slots
    behind = HALO + SPREAD
    right, left_feats = lax.optimization_barrier((by_column(right_feats), left_feats))
    left = lax.optimization_barrier(by_column(left_feats))
    before = passed(
        jnp.concatenate([right[col_count - behind :], left[col_count - HALO :]], axis=0), "lon", 1
    )
    right_before, left_before = before[:behind], before[behind:]
    after = passed(jnp.concatenate([right[:HALO], left[:HALO]], axis=0), "lon", -1)

    def partner(value, t):
        return lax.ppermute(value, "grp", [(i, i ^ t) for i in range(slots)]) if t > 0 else value

    def inner(target):
        return jnp.concatenate(
            [lax.dynamic_slice_in_dim(x, target * cols, cols, 0) for x in (right, left)], axis=0
        )

    inners = [partner(inner(me ^ t), t) for t in range(slots)]
    t1a, t1b, t2, t3 = banded_weights(w_first, w_second, w_out, slots)
    left_wide = jnp.concatenate([left_before, left, after[HALO:]], axis=0)
    right_wide = jnp.concatenate([right_before, right, after[:HALO]], axis=0)

    def outer(target):
        start = target * cols
        return jnp.concatenate(
            [
                lax.dynamic_slice_in_dim(right_wide, start, behind, 0),
                lax.dynamic_slice_in_dim(right_wide, start + behind + cols, HALO, 0),
                lax.dynamic_slice_in_dim(left_wide, start, HALO, 0),
                lax.dynamic_slice_in_dim(left_wide, start + HALO + cols, HALO, 0),
            ],
            axis=0,
        )

    outers = [partner(outer(me ^ t), t) for t in range(slots)]
    feats = [x for pair in zip(inners, outers) for x in pair]
    near = 2 * slots // PARTS
    acc = first_part(feats[:near], t1a, slots, cols)
    pieces = aggregate(feats[near:], t1b, t2, t3, acc, slots, cols)
    return assemble([partner(pieces[t], t) for t in range(slots)])


def solution(mesh):
    placed = (P("grp", "pairs", "lon"), P("grp", "pairs", "lon"), P(), P(), P())
    return jax.shard_map(
        per_device,
        mesh=mesh,
        in_specs=placed,
        out_specs=P(("pairs", "grp"), "lon"),
        check_vma=False,
    )
```

```python
import functools

import jax
import jax.numpy as jnp
from jax import lax
from jax.experimental import pallas as pl
from jax.experimental.pallas import tpu as pltpu
from jax.sharding import PartitionSpec as P

C = 320
G = 40
CH = 32
DISP = 48
PER = C // G
ROWS = 16
HALF = ROWS // 2
LANE = 128
HALO = 4
SPREAD = DISP - 1
PARTS = 2
SHARE = G * ROWS // PARTS
WHOLE = SHARE // LANE * LANE
REST = SHARE - WHOLE
DEPTH = 3 * WHOLE + 4 * REST
FIRST_OUT = ROWS * CH
PART = FIRST_OUT // 2
CAP = 12.0
CHUNKS = 7


def weights_kernel(
    w1_ref, w2_ref, w3_ref, t1a_ref, t1b_ref, t2_ref, t3_ref, v1, v3_ref, *, slots
):
    here = G // slots
    me = lax.axis_index("grp")
    quarters = LANE // CH
    for tap in range(27):
        w1 = w1_ref[tap].astype(jnp.float32)
        v1[tap, :, :] = jnp.transpose(jnp.concatenate([w1] * quarters, axis=0))
    row16 = lax.broadcasted_iota(jnp.int32, (ROWS, LANE), 0)
    quarter = lax.broadcasted_iota(jnp.int32, (ROWS, LANE), 1) // CH
    masks = []
    for q in range(FIRST_OUT // LANE):
        at = quarters * q + quarter
        out_row = 2 * (at % HALF) + at // HALF
        masks.append(
            [jnp.where(row16 == out_row + kh - 1, 1.0, 0.0).astype(jnp.bfloat16) for kh in range(3)]
        )
    per_part = slots // PARTS
    for part, t1_ref in enumerate((t1a_ref, t1b_ref)):
        for kw in range(3):

            def one_tap(t, carry):
                e, slot = t // per_part, t % per_part
                tap = (2 - e) * 9 + kw
                group = (me ^ (part * per_part + slot)) * here
                for i in range(here):
                    rows = []
                    for kh in range(3):
                        row = v1[tap + 3 * kh, pl.ds(group + i, 1), :]
                        rows.append(jnp.broadcast_to(row, (ROWS, LANE)).astype(jnp.bfloat16))
                    at = (slot * here + i) * ROWS
                    start = jnp.where(at < WHOLE, e * WHOLE + at, 3 * WHOLE + e * REST + at - WHOLE)
                    start = pl.multiple_of(start, ROWS)
                    for q in range(FIRST_OUT // LANE):
                        value = (
                            masks[q][0] * rows[0] + masks[q][1] * rows[1] + masks[q][2] * rows[2]
                        )
                        t1_ref[kw, pl.ds(start, ROWS), q * LANE : (q + 1) * LANE] = value
                return carry

            lax.fori_loop(0, 3 * per_part, one_tap, 0)
            t1_ref[kw, DEPTH - REST :, :] = jnp.zeros((REST, FIRST_OUT), jnp.bfloat16)

    lane32 = lax.broadcasted_iota(jnp.int32, (CH, LANE), 1) // CH
    for kw in range(3):
        for e in range(3):
            tap = (2 - e) * 9 + kw
            v2 = [
                jnp.transpose(
                    jnp.concatenate([w2_ref[tap + 3 * kh].astype(jnp.float32)] * quarters, axis=0)
                )
                for kh in range(3)
            ]
            for hi in range(HALF):
                for q in range(PART // LANE):
                    value = jnp.zeros((CH, LANE), jnp.float32)
                    for kh in range(3):
                        if quarters * q <= hi - kh + 1 < quarters * (q + 1):
                            value = jnp.where(quarters * q + lane32 == hi - kh + 1, v2[kh], value)
                    start = e * PART + hi * CH
                    t2_ref[kw, start : start + CH, q * LANE : (q + 1) * LANE] = value.astype(
                        jnp.bfloat16
                    )

    v3_ref[...] = jnp.zeros_like(v3_ref)
    for i in range(9):
        v3_ref[3 * i : 3 * i + 3, :CH] = w3_ref[i].astype(jnp.float32)
    taps = jnp.transpose(v3_ref[...])[:CH]
    out_lane = lax.broadcasted_iota(jnp.int32, (CH, LANE), 1)
    for kw in range(3):
        v3 = []
        for kh in range(3):
            value = jnp.zeros((CH, LANE), jnp.float32)
            for e in range(3):
                tap = (2 - e) * 9 + 3 * kh + kw
                column = jnp.broadcast_to(taps[:, tap : tap + 1], (CH, LANE))
                value = jnp.where(out_lane // ROWS == e, column, value)
            v3.append(value)
        for at in range(ROWS):
            hi = 2 * (at % HALF) + at // HALF
            value = jnp.zeros((CH, LANE), jnp.float32)
            for kh in range(3):
                value = jnp.where(out_lane % ROWS == hi - kh + 1, v3[kh], value)
            t3_ref[kw, at * CH : (at + 1) * CH, :] = value.astype(jnp.bfloat16)


def banded_weights(w_first, w_second, w_out, slots):
    w1 = jnp.transpose(w_first, (2, 3, 4, 0, 1)).reshape(27, CH, G)
    w2 = jnp.transpose(w_second, (2, 3, 4, 0, 1)).reshape(27, CH, CH)
    w3 = jnp.transpose(w_out, (0, 2, 3, 4, 1)).reshape(9, 3, CH)
    whole = pl.BlockSpec(memory_space=pltpu.VMEM)
    shapes = [
        (3, DEPTH, FIRST_OUT),
        (3, DEPTH, FIRST_OUT),
        (3, 3 * PART, PART),
        (3, FIRST_OUT, LANE),
    ]
    return pl.pallas_call(
        functools.partial(weights_kernel, slots=slots),
        out_shape=tuple(jax.ShapeDtypeStruct(shape, jnp.bfloat16) for shape in shapes),
        in_specs=[whole, whole, whole],
        out_specs=[whole] * 4,
        scratch_shapes=[
            pltpu.VMEM((27, G, LANE), jnp.float32),
            pltpu.VMEM((LANE, LANE), jnp.float32),
        ],
        compiler_params=pltpu.CompilerParams(vmem_limit_bytes=8 << 20),
        cost_estimate=pl.CostEstimate(flops=9_000_000, bytes_accessed=8_000_000, transcendentals=0),
        name="banded_weights",
    )(w1, w2, w3)


def unpack(feats, left, right, slots, cols):
    span = G // slots * ROWS
    blocks = WHOLE // LANE
    behind = HALO + SPREAD

    def joined(refs, k):
        pieces = [ref[:, k * span : (k + 1) * span].astype(jnp.float32) for ref in refs]
        pieces.append(jnp.zeros((pieces[0].shape[0], LANE - REST), jnp.float32))
        return jnp.concatenate(pieces, axis=1)

    for k in range(PER):
        inner, outer = joined(feats[0::2], k), joined(feats[1::2], k)
        for j in range(blocks + 1):
            at = k * (blocks + 1) + j
            mine = inner[:, j * LANE : (j + 1) * LANE]
            edge = outer[:, j * LANE : (j + 1) * LANE]
            right[at, :behind, :] = edge[:behind]
            right[at, behind : behind + cols, :] = mine[:cols]
            right[at, behind + cols :, :] = edge[behind : behind + HALO]
            left[at, :HALO, :] = edge[behind + HALO : behind + 2 * HALO]
            left[at, HALO : HALO + cols, :] = mine[cols:]
            left[at, HALO + cols :, :] = edge[behind + 2 * HALO :]


def cost_columns(first_column, last_column, left, right, cells, cost_pad):
    blocks = WHOLE // LANE
    for w in range(first_column, last_column):
        rows = slice(w * DISP, (w + 1) * DISP)
        for j in range(blocks + 1):
            total = None
            for k in range(PER):
                at = k * (blocks + 1) + j
                l_row = jnp.broadcast_to(left[at, w : w + 1, :], (DISP, LANE))
                term = l_row * right[at, w : w + DISP, :]
                total = term if total is None else total + term
            total = (total * (1.0 / PER)).astype(jnp.bfloat16)
            wide = total.astype(jnp.float32)
            pad = cost_pad.at[w % 2, j]
            pad[8 : 8 + DISP, :] = wide
            moved = [pad[7 : 7 + DISP, :], wide, pad[9 : 9 + DISP, :]]
            if j < blocks:
                for e in range(3):
                    lanes = e * WHOLE + j * LANE
                    cells[rows, lanes : lanes + LANE] = moved[e].astype(jnp.bfloat16)
            else:
                pair = moved[0] + pltpu.roll(moved[1], REST, 1)
                lanes = 3 * WHOLE
                cells[rows, lanes : lanes + LANE] = pair.astype(jnp.bfloat16)
                lanes += LANE
                cells[rows, lanes : lanes + LANE] = moved[2].astype(jnp.bfloat16)


def bounds_of(count, chunks):
    return [count * i // chunks for i in range(chunks + 1)]


def first_kernel(*refs, slots, cols):
    count = 2 * slots // PARTS
    t1_ref, acc, left, right, cells, cost_pad = refs[count:]
    unpack(refs[:count], left, right, slots, cols)
    cost_pad[...] = jnp.zeros_like(cost_pad)
    bounds = bounds_of(cols + 6, CHUNKS)
    cost_columns(0, bounds[1] + 2, left, right, cells, cost_pad)
    for i in range(CHUNKS):
        if i + 1 < CHUNKS:
            cost_columns(bounds[i + 1] + 2, bounds[i + 2] + 2, left, right, cells, cost_pad)
        low, high = bounds[i], bounds[i + 1]
        total = None
        for kw in range(3):
            term = jnp.dot(
                cells[(low + kw) * DISP : (high + kw) * DISP, :],
                t1_ref[kw],
                preferred_element_type=jnp.float32,
            )
            total = term if total is None else total + term
        acc[low * DISP : high * DISP, :] = total


def main_kernel(*refs, slots, cols):
    count = 2 * slots // PARTS
    t1_ref, t2_ref, t3_ref, acc_ref = refs[count : count + 4]
    outs = refs[count + 4 : count + 4 + slots]
    (
        left, right, cells, cost_pad, acc, first, first_pad, second, score_pad, out_pad,
    ) = refs[count + 4 + slots :]
    unpack(refs[:count], left, right, slots, cols)
    cost_pad[...] = jnp.zeros_like(cost_pad)
    first_pad[...] = jnp.zeros_like(first_pad)
    bounds = bounds_of(cols + 6, CHUNKS)
    cost_columns(0, bounds[1] + 2, left, right, cells, cost_pad)
    for i in range(CHUNKS):
        if i + 1 < CHUNKS:
            cost_columns(bounds[i + 1] + 2, bounds[i + 2] + 2, left, right, cells, cost_pad)
        low, high = bounds[i], bounds[i + 1]
        total = acc_ref[low * DISP : high * DISP, :]
        for kw in range(3):
            total = total + jnp.dot(
                cells[(low + kw) * DISP : (high + kw) * DISP, :],
                t1_ref[kw],
                preferred_element_type=jnp.float32,
            )
        acc[low * DISP : high * DISP, :] = total
        for w in range(low, high):
            rows = slice(w * DISP, (w + 1) * DISP)
            for q in range(FIRST_OUT // LANE):
                value = acc[rows, q * LANE : (q + 1) * LANE]
                value = jnp.maximum(value, 0.0).astype(jnp.bfloat16)
                pad = first_pad.at[w % 2, q]
                pad[8 : 8 + DISP, :] = value.astype(jnp.float32)
                for e in range(3):
                    lanes = (q // 2) * 3 * PART + e * PART + (q % 2) * LANE
                    if e == 1:
                        moved = value
                    else:
                        moved = pad[6 + 2 * e : 6 + 2 * e + DISP, :].astype(jnp.bfloat16)
                    first[rows, lanes : lanes + LANE] = moved

    chunks = 6 if (cols + 2) % 6 == 0 else 2
    chunk = (cols + 2) // chunks
    for part in range(chunks):
        for p in range(2):
            lanes = p * 3 * PART
            total = None
            for kw in range(3):
                start = (part * chunk + 2 * kw) * DISP
                term = jnp.dot(
                    first[start : start + chunk * DISP, lanes : lanes + 3 * PART],
                    t2_ref[kw],
                    preferred_element_type=jnp.float32,
                )
                total = term if total is None else total + term
            start = (part * chunk + 2) * DISP
            kept = first[start : start + chunk * DISP, lanes + PART : lanes + 2 * PART]
            total = jnp.maximum(total + kept.astype(jnp.float32), 0.0).astype(jnp.bfloat16)
            start = part * chunk * DISP
            second[start : start + chunk * DISP, p * PART : (p + 1) * PART] = total

    total = None
    for kw in range(3):
        term = jnp.dot(
            second[kw * DISP : (kw + cols) * DISP, :], t3_ref[kw], preferred_element_type=jnp.float32
        )
        total = term if total is None else total + term
    score_pad[8 : 8 + cols * DISP, :] = total
    row = lax.broadcasted_iota(jnp.int32, (DISP, LANE), 0)
    level = ((DISP - 1) - row).astype(jnp.float32)

    def score_column(w, carry):
        base = pl.multiple_of(8 + w * DISP, 8)
        score = jnp.where(row == 0, 0.0, score_pad[pl.ds(base - 1, DISP), :])
        score = score + pltpu.roll(score_pad[pl.ds(base, DISP), :], LANE - ROWS, 1)
        later = jnp.where(row == DISP - 1, 0.0, score_pad[pl.ds(base + 1, DISP), :])
        score = score + pltpu.roll(later, LANE - 2 * ROWS, 1)
        weights = jnp.exp(CAP * jnp.tanh(score / CAP))
        bottom = jnp.sum(weights, axis=0, keepdims=True)
        top = jnp.sum(weights * level, axis=0, keepdims=True)
        out_pad[pl.ds(w, 1), :] = top / bottom / DISP
        return carry

    out_pad[...] = jnp.zeros_like(out_pad)
    score_pad[:8, :] = jnp.zeros((8, LANE), jnp.float32)
    score_pad[8 + cols * DISP :, :] = jnp.zeros((8, LANE), jnp.float32)
    lax.fori_loop(0, cols, score_column, 0, unroll=True)
    out_pad[...] = jnp.transpose(out_pad[...])
    me = lax.axis_index("grp")
    share = ROWS // slots
    for t in range(slots):
        outs[t][...] = out_pad[pl.ds((me ^ t) * share, share), :cols]


def scratch(cols):
    cost_cols = cols + 2 * HALO
    tiles = PER * (WHOLE // LANE + 1)
    return [
        pltpu.VMEM((tiles, cost_cols, LANE), jnp.float32),
        pltpu.VMEM((tiles, cost_cols + SPREAD, LANE), jnp.float32),
        pltpu.VMEM((cost_cols * DISP, DEPTH), jnp.bfloat16),
        pltpu.VMEM((2, WHOLE // LANE + 1, DISP + 16, LANE), jnp.float32),
    ]


def first_part(feats, t1, slots, cols):
    whole = pl.BlockSpec(memory_space=pltpu.VMEM)
    return pl.pallas_call(
        functools.partial(first_kernel, slots=slots, cols=cols),
        out_shape=jax.ShapeDtypeStruct(((cols + 6) * DISP, FIRST_OUT), jnp.float32),
        in_specs=[whole] * (len(feats) + 1),
        out_specs=whole,
        scratch_shapes=scratch(cols),
        compiler_params=pltpu.CompilerParams(vmem_limit_bytes=16 << 20),
        cost_estimate=pl.CostEstimate(
            flops=7_000_000_000, bytes_accessed=6_000_000, transcendentals=0
        ),
        name="first_part",
    )(*feats, t1)


def aggregate(feats, t1, t2, t3, acc, slots, cols):
    whole = pl.BlockSpec(memory_space=pltpu.VMEM)
    return pl.pallas_call(
        functools.partial(main_kernel, slots=slots, cols=cols),
        out_shape=[jax.ShapeDtypeStruct((ROWS // slots, cols), jnp.float32)] * slots,
        in_specs=[whole] * (len(feats) + 4),
        out_specs=[whole] * slots,
        scratch_shapes=scratch(cols)
        + [
            pltpu.VMEM(((cols + 6) * DISP, FIRST_OUT), jnp.float32),
            pltpu.VMEM(((cols + 6) * DISP, 3 * FIRST_OUT), jnp.bfloat16),
            pltpu.VMEM((2, FIRST_OUT // LANE, DISP + 16, LANE), jnp.float32),
            pltpu.VMEM(((cols + 2) * DISP, FIRST_OUT), jnp.bfloat16),
            pltpu.VMEM((cols * DISP + 16, LANE), jnp.float32),
            pltpu.VMEM((LANE, LANE), jnp.float32),
        ],
        compiler_params=pltpu.CompilerParams(vmem_limit_bytes=20 << 20),
        name="aggregate",
    )(*feats, t1, t2, t3, acc)


def assemble_kernel(*refs, slots):
    me = lax.axis_index("grp")
    pieces = [ref[...] for ref in refs[:slots]]
    bit = 1
    while bit < slots:
        swap = (me & bit) > 0
        pieces = [jnp.where(swap, pieces[t ^ bit], pieces[t]) for t in range(slots)]
        bit *= 2
    cols = pieces[0].shape[1]
    for t in range(slots):
        refs[slots][:, t * cols : (t + 1) * cols] = pieces[t]


def assemble(pieces):
    slots = len(pieces)
    rows, cols = pieces[0].shape
    whole = pl.BlockSpec(memory_space=pltpu.VMEM)
    return pl.pallas_call(
        functools.partial(assemble_kernel, slots=slots),
        out_shape=jax.ShapeDtypeStruct((rows, cols * slots), jnp.float32),
        in_specs=[whole] * slots,
        out_specs=whole,
        compiler_params=pltpu.CompilerParams(vmem_limit_bytes=4 << 20),
        name="assemble",
    )(*pieces)


def by_column(block):
    channels, row_count, col_count = block.shape
    grouped = block.reshape(channels // PER, PER, row_count, col_count)
    return jnp.transpose(grouped, (3, 1, 0, 2)).reshape(col_count, channels * row_count)


def passed(value, axis, by):
    peers = lax.axis_size(axis)
    return lax.ppermute(value, axis, [(i, (i + by) % peers) for i in range(peers)])


def per_device(left_feats, right_feats, w_first, w_second, w_out):
    _, row_count, col_count = left_feats.shape
    slots = lax.axis_size("grp")
    me = lax.axis_index("grp")
    cols = col_count // slots
    behind = HALO + SPREAD
    right, left_feats = lax.optimization_barrier((by_column(right_feats), left_feats))
    left = lax.optimization_barrier(by_column(left_feats))
    before = passed(
        jnp.concatenate([right[col_count - behind :], left[col_count - HALO :]], axis=0), "lon", 1
    )
    right_before, left_before = before[:behind], before[behind:]
    after = passed(jnp.concatenate([right[:HALO], left[:HALO]], axis=0), "lon", -1)

    def partner(value, t):
        return lax.ppermute(value, "grp", [(i, i ^ t) for i in range(slots)]) if t > 0 else value

    def inner(target):
        return jnp.concatenate(
            [lax.dynamic_slice_in_dim(x, target * cols, cols, 0) for x in (right, left)], axis=0
        )

    inners = [partner(inner(me ^ t), t) for t in reversed(range(slots))][::-1]
    t1a, t1b, t2, t3 = banded_weights(w_first, w_second, w_out, slots)
    left_wide = jnp.concatenate([left_before, left, after[HALO:]], axis=0)
    right_wide = jnp.concatenate([right_before, right, after[:HALO]], axis=0)

    def outer(target):
        start = target * cols
        return jnp.concatenate(
            [
                lax.dynamic_slice_in_dim(right_wide, start, behind, 0),
                lax.dynamic_slice_in_dim(right_wide, start + behind + cols, HALO, 0),
                lax.dynamic_slice_in_dim(left_wide, start, HALO, 0),
                lax.dynamic_slice_in_dim(left_wide, start + HALO + cols, HALO, 0),
            ],
            axis=0,
        )

    outers = [partner(outer(me ^ t), t) for t in reversed(range(slots))][::-1]
    feats = [x for pair in zip(inners, outers) for x in pair]
    near = 2 * slots // PARTS
    acc = first_part(feats[:near], t1a, slots, cols)
    pieces = aggregate(feats[near:], t1b, t2, t3, acc, slots, cols)
    return assemble([partner(pieces[t], t) for t in range(slots)])


def solution(mesh):
    placed = (P("grp", "pairs", "lon"), P("grp", "pairs", "lon"), P(), P(), P())
    return jax.shard_map(
        per_device,
        mesh=mesh,
        in_specs=placed,
        out_specs=P(("pairs", "grp"), "lon"),
        check_vma=False,
    )
```
